32 devices in a mesh: groups: 2 (over y), tm: 4 (over z), tile: 2 (over x), chan: 2 (over core).
Axes of the slice: x: 2, y: 2, z: 4, core: 2. Of those that a mesh axis runs over, the one named last changes fastest.
Arguments:
- latent: bfloat16 [16, 24, 32, 512], P(('groups', 'tm'), None, 'tile', 'chan'), parts along dimension 0, may hold values from -110 to 110
- gn_gain: bfloat16 [512], P('chan'), may hold values from 0.099609375 to 1.8984375
- gn_bias: bfloat16 [512], P('chan'), may hold values from -3 to 3
- conv_weight: bfloat16 [27, 512, 512], P(None, 'tm', 'chan'), may hold values from -0.0546875 to 0.0546875
- conv_bias: bfloat16 [512], P('chan'), may hold values from -3 to 3
Outputs:
- decoded: bfloat16 [16, 24, 32, 512], P(('groups', 'tm'), None, 'tile', 'chan'), parts along dimension 0
The draws below stay inside these ranges and needn't reach their ends.
There are 2 independent parts, one for each index of `groups`. The reference program is written for one: setup_inputs(seed, part) draws one part's arguments, and reference() takes and returns one part's arrays. A program takes and returns all parts, laid end to end along the dimension named above; an argument that names none is the same for every part. Nothing has to cross between parts.
All inputs are finite; a program needn't handle non-finite values.
Results may differ from the reference program's by a relative error of at most 0.0043.
Values may be sent and summed in bfloat16 or wider, within the bound.
No kernel may reach another device: no remote copies, remote signals or barrier semaphores. Data moves between devices by JAX's collectives and lax.ppermute only.
A program may use at most 128 MiB of HBM per device.

```python
import math
import jax
import jax.numpy as jnp
from jax import lax

CH = 512
GROUPS = 32
ROWS = 24
FRAMES = 8
WIDTH = 32


def draw_latent(key, part):
    noise_key, chan_key, pos_key = jax.random.split(jax.random.fold_in(key, 7), 3)
    shape = (FRAMES, ROWS, WIDTH, CH)
    noise = jnp.clip(jax.random.normal(noise_key, shape, jnp.float32), -4.0, 4.0)
    rise = math.sqrt(3.0)
    chan_scale = jnp.exp(jax.random.uniform(chan_key, (CH,), jnp.float32, math.log(0.3), math.log(3.0)))
    pos_scale = jnp.exp(jax.random.uniform(pos_key, (ROWS, WIDTH), jnp.float32, math.log(0.5), math.log(2.0)))
    frame_pos = jnp.arange(FRAMES, dtype=jnp.float32) / max(FRAMES - 1, 1)
    col_pos = jnp.arange(WIDTH, dtype=jnp.float32) / max(WIDTH - 1, 1)
    slopes = (rise ** frame_pos)[:, None, None, None] * (rise ** col_pos)[None, None, :, None]
    values = noise * chan_scale * pos_scale[None, :, :, None] * slopes
    return values.astype(jnp.bfloat16)


def block_levels(own_key, dims, shards, low, top_value):
    def one(dim, shards_of):
        steps = jax.random.uniform(jax.random.fold_in(jax.random.fold_in(own_key, 6), dim), (shards_of,), jnp.float32, low / len(shards), top_value / len(shards))
        return jnp.repeat(jnp.exp(steps), dims[dim] // shards_of).reshape((-1,) + (1,) * (len(dims) - dim - 1))

    loudness = one(*shards[0])
    for cut in shards[1:]:
        loudness = loudness * one(*cut)
    return loudness


def gaussian(stream_key, shape, width, bound, pieces=(), kind=jnp.bfloat16):
    values = jax.random.normal(stream_key, shape, jnp.float32) * width
    if len(pieces) > 0:
        values = block_levels(stream_key, shape, pieces, -0.22, 0.18) * values
    return jnp.clip(values, min=-bound, max=bound).astype(kind)


def setup_inputs(seed: int = 0, part: int = 0) -> dict:
    key_of = jax.random.split(jax.random.key(seed), 6)
    part_splits = jax.random.split(jax.random.fold_in(key_of[5], part), 6)
    latent = draw_latent(jax.random.fold_in(jax.random.fold_in(key_of[5], part), 71), part)
    gn_gain = jnp.clip(1.0 + 0.18 * jax.random.normal(key_of[1], (CH,), jnp.float32), 0.099609375, 1.8984375).astype(jnp.bfloat16)
    gn_bias = gaussian(key_of[2], (CH,), 0.5, 3.0, ((0, 2),))
    conv_weight = gaussian(key_of[3], (27, CH, CH), (27 * CH) ** -0.5, 0.0546875, ((1, 4), (2, 2)))
    conv_bias = gaussian(key_of[4], (CH,), 0.5, 3.0, ((0, 2),))
    return {"latent": latent, "gn_gain": gn_gain, "gn_bias": gn_bias, "conv_weight": conv_weight, "conv_bias": conv_bias}


def normalize(latent, gn_gain, gn_bias):
    values = latent.astype(jnp.float32)
    group_ch = CH // GROUPS
    shaped = values.reshape(values.shape[0], values.shape[1], values.shape[2], GROUPS, group_ch)
    entries = values.shape[0] * values.shape[1] * values.shape[2] * group_ch
    mean_grp = lax.optimization_barrier(jnp.sum(shaped, axis=(0, 1, 2, 4))) / entries
    square_grp = lax.optimization_barrier(jnp.sum(shaped * shaped, axis=(0, 1, 2, 4))) / entries
    inv_grp = lax.rsqrt(square_grp - mean_grp * mean_grp + 1e-06)
    mean_ch = jnp.repeat(mean_grp, group_ch)
    inv_ch = jnp.repeat(inv_grp, group_ch)
    scaled = (values - mean_ch) * inv_ch * gn_gain.astype(jnp.float32) + gn_bias.astype(jnp.float32)
    return jax.nn.silu(scaled).astype(jnp.bfloat16)

def reference(latent, gn_gain, gn_bias, conv_weight, conv_bias):
    normed = normalize(latent, gn_gain, gn_bias)
    inputs = normed.astype(jnp.float32)[None]
    kernel = conv_weight.astype(jnp.float32).reshape(3, 3, 3, CH, CH)
    output = lax.conv_general_dilated(inputs, kernel, (1, 1, 1), ((2, 0), (1, 1), (1, 1)), dimension_numbers=('NDHWC', 'DHWIO', 'NDHWC'), precision=lax.Precision.HIGHEST)
    return (output[0] + conv_bias.astype(jnp.float32)).astype(jnp.bfloat16)
```

```python
import functools

import jax
import jax.numpy as jnp
from jax import lax
from jax.experimental import pallas as pl
from jax.experimental.pallas import tpu as pltpu
from jax.sharding import PartitionSpec as P

CH = 512
GROUPS = 32
EPS = 1e-06
LANES = 128
VMEM = 48 << 20
STAT_ROWS = 16


def shifted(block, axis, distance):
    devices = range(lax.axis_size(axis))
    route = [(i - distance, i) for i in devices if i - distance in devices]
    return lax.ppermute(block, axis, route)


def extended_2(cells, sides, width):
    for axis, dim in sides:
        count = lax.axis_size(axis)
        ends = count - 1
        head = lax.slice_in_dim(cells, 0, width, axis=dim)
        tail = lax.slice_in_dim(cells, cells.shape[dim] - width, cells.shape[dim], axis=dim)
        cells = jnp.concatenate(
            [
                lax.ppermute(tail, axis, [(i, (i + 1) % count) for i in range(ends)]),
                cells,
                lax.ppermute(head, axis, [((i + 1) % count, i) for i in range(ends)]),
            ],
            axis=dim,
        )
    return cells


def normalize(latent, gn_gain, gn_bias):
    values = latent.astype(jnp.float32)
    n_frames, n_rows, n_cols, n_chans = latent.shape
    group_ch = CH // GROUPS
    local_groups = n_chans // group_ch
    shaped = values.reshape(n_frames, n_rows, n_cols, local_groups, group_ch)
    part_sum = jnp.sum(shaped, axis=(0, 1, 2, 4))
    part_square = jnp.sum(shaped * shaped, axis=(0, 1, 2, 4))
    total_sum, total_square = lax.psum((part_sum, part_square), ("tm", "tile"))
    entries = n_frames * n_rows * n_cols * group_ch * lax.axis_size("tm") * lax.axis_size("tile")
    mean_grp = total_sum / entries
    square_grp = total_square / entries
    inv_grp = lax.rsqrt(square_grp - mean_grp * mean_grp + 1e-06)
    mean_ch = jnp.repeat(mean_grp, group_ch)
    inv_ch = jnp.repeat(inv_grp, group_ch)
    scaled = (values - mean_ch) * inv_ch * gn_gain.astype(jnp.float32) + gn_bias.astype(jnp.float32)
    return jax.nn.silu(scaled).astype(jnp.bfloat16)


def conv_term(padded, n_frames, n_rows, n_cols, block_in):
    width_in = block_in.shape[1]
    columns = [
        padded[
            time_off : time_off + n_frames, row_off : row_off + n_rows, col_off : col_off + n_cols
        ]
        for time_off in range(3)
        for row_off in range(3)
        for col_off in range(3)
    ]
    stacked = jnp.stack(columns, axis=3).reshape(n_frames * n_rows * n_cols, 27 * width_in)
    matrix = block_in.reshape(27 * width_in, block_in.shape[2])
    return jnp.dot(stacked, matrix, preferred_element_type=jnp.float32)


def body(latent, gn_gain, gn_bias, conv_weight, conv_bias):
    n_frames, n_rows, n_cols, n_chans = latent.shape
    normed = normalize(latent, gn_gain, gn_bias)
    full_feat = lax.all_gather(normed, "chan", axis=3, tiled=True)
    earlier = shifted(full_feat, "tm", 1)
    extended = jnp.concatenate([earlier, full_feat], axis=0)
    rimmed = extended_2(extended, (("tile", 2),), 1)
    padded = jnp.pad(rimmed, ((0, 0), (1, 1), (0, 0), (0, 0)))
    summed = conv_term(
        padded, n_frames, n_rows, n_cols, lax.all_gather(conv_weight, "tm", axis=1, tiled=True)
    )
    result = (summed + conv_bias.astype(jnp.float32)).astype(jnp.bfloat16)
    return result.reshape(n_frames, n_rows, n_cols, n_chans)


def near_of(s):
    return s + 1 - 2 * (s % 2)


def mid_of(s):
    return (s + 2) % 4


def far_of(s):
    return 3 - s


def edges_kernel(latent_ref, out_ref, wide_ref, *, cells, cols):
    wide = latent_ref[...].astype(jnp.float32)
    edges = cells // cols
    first = jnp.where(lax.axis_index("tile") == 0, cols - 1, 0)
    for k in range(wide.shape[1] // LANES):
        lanes = slice(k * LANES, (k + 1) * LANES)
        wide_ref[...] = wide[:, lanes]
        out_ref[:edges, lanes] = wide_ref[pl.ds(first, edges, stride=cols), :]
    total = jnp.sum(wide, axis=0, keepdims=True)
    square = jnp.sum(wide * wide, axis=0, keepdims=True)
    out_ref[edges:] = jnp.concatenate([total, square, jnp.zeros((6, wide.shape[1]), jnp.float32)], axis=0)


def three(value):
    high = value.astype(jnp.bfloat16)
    rest = value - high.astype(jnp.float32)
    mid = rest.astype(jnp.bfloat16)
    low = (rest - mid.astype(jnp.float32)).astype(jnp.bfloat16)
    return [high, mid, low]


def pack_kernel(latent_ref, own_ref, other_ref, gain_ref, bias_ref, same_ref, next_ref, *, cells, edges):
    sums = own_ref[edges : edges + 2] + other_ref[edges : edges + 2]
    tail = three(sums[0:1]) + three(sums[1:2]) + [gain_ref[...], bias_ref[...]]
    tail = jnp.concatenate([row.astype(jnp.float32) for row in tail], axis=0)
    tail = jnp.concatenate([tail, jnp.zeros_like(tail)], axis=0).astype(jnp.bfloat16)
    edge = other_ref[:edges].astype(jnp.bfloat16)

    def fill(out_ref, block):
        lanes = slice(block * LANES, (block + 1) * LANES)
        out_ref[:cells] = latent_ref[:, lanes]
        out_ref[cells : cells + edges] = edge[:, lanes]
        out_ref[cells + edges :] = tail[:, lanes]

    parity = lax.axis_index("tm") % 2

    @pl.when(parity == 0)
    def _():
        fill(same_ref, 0)
        fill(next_ref, 1)

    @pl.when(parity == 1)
    def _():
        fill(same_ref, 1)
        fill(next_ref, 0)


def group_total(row, group_ch):
    lane = lax.broadcasted_iota(jnp.int32, row.shape, 1)
    step = 1
    while step < group_ch:
        up = pltpu.roll(row, LANES - step, 1)
        down = pltpu.roll(row, step, 1)
        row = row + jnp.where((lane // step) % 2 == 0, up, down)
        step *= 2
    return row


def spread_kernel(same_ref, a_ref, b_ref, c_ref, d_ref, out_ref, own_ref, *, frames, rows, cols, entries):
    s = lax.axis_index("tm")
    home = lax.axis_index("chan") == s // 2
    tile = lax.axis_index("tile")
    cells = frames * rows * cols
    edges = frames * rows
    base = cells + edges

    @pl.when(home)
    def _():
        own_ref[...] = same_ref[...]

    @pl.when(jnp.logical_not(home))
    def _():
        own_ref[...] = d_ref[...]

    near, mid, far = near_of(s), mid_of(s), far_of(s)
    pieces = (
        (own_ref, jnp.where(home, s, mid)),
        (a_ref, jnp.where(home, near, far)),
        (b_ref, jnp.where(home, mid, s)),
        (c_ref, jnp.where(home, far, near)),
    )
    tails = [ref[base : base + STAT_ROWS].astype(jnp.float32) for ref, _ in pieces]
    stats = tails[0] + tails[1] + tails[2] + tails[3]
    total = group_total(stats[0:1] + stats[1:2] + stats[2:3], CH // GROUPS) / entries
    square = group_total(stats[3:4] + stats[4:5] + stats[5:6], CH // GROUPS) / entries
    scale = lax.rsqrt(square - total * total + EPS) * tails[0][6:7]
    shift = tails[0][7:8]

    def normed(raw):
        value = (raw.astype(jnp.float32) - total) * scale + shift
        return value / (1.0 + jnp.exp(-value))

    n_all = out_ref.shape[1]
    zero_row = jnp.zeros((cols, LANES), jnp.bfloat16)
    for d in range(3):
        for f in range(n_all):
            out_ref[d, f, 0] = zero_row
            out_ref[d, f, rows + 1] = zero_row
        for f in range(2):
            out_ref[d, f, 1 : rows + 1] = jnp.zeros((rows, cols, LANES), jnp.bfloat16)
    col = lax.broadcasted_iota(jnp.int32, (rows, cols, LANES), 1)
    span = rows * cols
    for ref, block in pieces:
        for f in range(frames):
            value = normed(ref[f * span : (f + 1) * span])
            edge = normed(ref[cells + f * rows : cells + (f + 1) * rows])
            edge = jnp.broadcast_to(edge[:, None, :], (rows, cols, LANES))
            left = pltpu.roll(value, 1, 0).reshape(rows, cols, LANES)
            left = jnp.where(col == 0, jnp.where(tile == 1, edge, 0.0), left)
            right = pltpu.roll(value, span - 1, 0).reshape(rows, cols, LANES)
            right = jnp.where(col == cols - 1, jnp.where(tile == 0, edge, 0.0), right)
            at = 2 + block * frames + f
            out_ref[0, at, 1 : rows + 1] = left.astype(jnp.bfloat16)
            out_ref[1, at, 1 : rows + 1] = value.reshape(rows, cols, LANES).astype(jnp.bfloat16)
            out_ref[2, at, 1 : rows + 1] = right.astype(jnp.bfloat16)


def partial_kernel(spread_ref, weight_ref, *rest, block_of, frame_list, frames, rows, cols, adds, with_bias):
    out_ref = rest[-1]
    block = block_of(lax.axis_index("tm"))
    span = rows * cols
    for k, f in enumerate(frame_list):
        at = block * frames + f
        stacked = jnp.concatenate(
            [
                spread_ref[d, at + a, b : b + rows].reshape(span, LANES)
                for a in range(3)
                for b in range(3)
                for d in range(3)
            ],
            axis=1,
        )
        total = jnp.dot(stacked, weight_ref[...], preferred_element_type=jnp.float32)
        here = slice(k * span, (k + 1) * span)
        for ref in rest[:adds]:
            total = total + ref[here].astype(jnp.float32)
        if with_bias:
            total = total + rest[adds][...].astype(jnp.float32)
        out_ref[here] = total.astype(out_ref.dtype)


def params():
    return pltpu.CompilerParams(vmem_limit_bytes=VMEM)


def split_body(latent, gn_gain, gn_bias, conv_weight, conv_bias):
    frames, rows, cols, chans = latent.shape
    outs = conv_weight.shape[2]
    cells = frames * rows * cols
    edges = frames * rows
    n_blocks = lax.axis_size("tm")
    entries = cells * n_blocks * lax.axis_size("tile") * (CH // GROUPS)
    flat = latent.reshape(cells, chans)

    own = pl.pallas_call(
        functools.partial(edges_kernel, cells=cells, cols=cols),
        out_shape=jax.ShapeDtypeStruct((edges + 8, chans), jnp.float32),
        scratch_shapes=[pltpu.VMEM((cells, LANES), jnp.float32)],
        compiler_params=params(),
    )(flat)
    other = lax.ppermute(own, "tile", [(0, 1), (1, 0)])
    packed = jax.ShapeDtypeStruct((cells + edges + STAT_ROWS, LANES), jnp.bfloat16)
    same, following = pl.pallas_call(
        functools.partial(pack_kernel, cells=cells, edges=edges),
        out_shape=(packed, packed),
        compiler_params=params(),
    )(flat, own, other, gn_gain.reshape(1, chans), gn_bias.reshape(1, chans))

    both = ("tm", "chan")
    route_a, route_b, route_d = [], [], []
    for s in range(n_blocks):
        h = s // 2
        route_a += [(2 * s + h, 2 * near_of(s) + h), (2 * s + 1 - h, 2 * far_of(s) + h)]
        route_b += [(2 * s + h, 2 * s + 1 - h), (2 * s + 1 - h, 2 * mid_of(s) + 1 - h)]
        route_d += [(2 * s + h, 2 * s + 1 - h)]
    got_a = lax.ppermute(following, both, route_a)
    got_b = lax.ppermute(same, both, route_b)
    got_c = lax.ppermute(got_a, "chan", [(0, 1), (1, 0)])
    got_d = lax.ppermute(got_b, both, route_d)
    spread = pl.pallas_call(
        functools.partial(spread_kernel, frames=frames, rows=rows, cols=cols, entries=entries),
        out_shape=jax.ShapeDtypeStruct((3, n_blocks * frames + 2, rows + 2, cols, LANES), jnp.bfloat16),
        scratch_shapes=[pltpu.VMEM(packed.shape, jnp.bfloat16)],
        compiler_params=params(),
    )(same, got_a, got_b, got_c, got_d)

    weight = conv_weight.reshape(27 * LANES, outs)
    bias = conv_bias.reshape(1, outs)

    def partial_sum(block_of, frame_list, adds=(), with_bias=False, dtype=jnp.bfloat16):
        size = len(frame_list) * rows * cols
        return pl.pallas_call(
            functools.partial(
                partial_kernel,
                block_of=block_of,
                frame_list=frame_list,
                frames=frames,
                rows=rows,
                cols=cols,
                adds=len(adds),
                with_bias=with_bias,
            ),
            out_shape=jax.ShapeDtypeStruct((size, outs), dtype),
            compiler_params=params(),
            cost_estimate=pl.CostEstimate(
                flops=2 * size * 27 * LANES * outs, transcendentals=0, bytes_accessed=4 * size * outs
            ),
        )(spread, weight, *adds, *([bias] if with_bias else []))

    near_route = [(s, near_of(s)) for s in range(n_blocks)]
    far_route = [(s, far_of(s)) for s in range(n_blocks)]
    beyond = [
        lax.ppermute(partial_sum(lambda s: far_of(near_of(s)), (f,)), "tm", near_route) for f in range(frames)
    ]
    arrived = [
        lax.ppermute(partial_sum(far_of, (f,), (beyond[f],)), "tm", far_route) for f in range(frames)
    ]
    beside = lax.ppermute(partial_sum(near_of, tuple(range(frames))), "tm", near_route)
    home = partial_sum(lambda s: s, tuple(range(frames)), (beside,), True, jnp.float32)
    result = home + jnp.concatenate(arrived, axis=0).astype(jnp.float32)
    return result.astype(jnp.bfloat16).reshape(frames, rows, cols, outs)


def splits(mesh):
    size = mesh.shape
    return size["tm"] == 4 and size["tile"] == 2 and size["chan"] == 2 and CH == size["tm"] * LANES


def solution(mesh):
    in_specs = (
        P(("groups", "tm"), None, "tile", "chan"),
        P("chan"),
        P("chan"),
        P(None, "tm", "chan"),
        P("chan"),
    )
    out_specs = P(("groups", "tm"), None, "tile", "chan")
    chosen = split_body if splits(mesh) else body
    return jax.shard_map(chosen, mesh=mesh, in_specs=in_specs, out_specs=out_specs, check_vma=False)
```

```python
import functools

import jax
import jax.numpy as jnp
from jax import lax
from jax.experimental import pallas as pl
from jax.experimental.pallas import tpu as pltpu
from jax.sharding import PartitionSpec as P

CH = 512
GROUPS = 32
EPS = 1e-06
LANES = 128
VMEM = 48 << 20
STAT_ROWS = 16


def shifted(block, axis, distance):
    devices = range(lax.axis_size(axis))
    route = [(i - distance, i) for i in devices if i - distance in devices]
    return lax.ppermute(block, axis, route)


def extended_2(cells, sides, width):
    for axis, dim in sides:
        count = lax.axis_size(axis)
        ends = count - 1
        head = lax.slice_in_dim(cells, 0, width, axis=dim)
        tail = lax.slice_in_dim(cells, cells.shape[dim] - width, cells.shape[dim], axis=dim)
        cells = jnp.concatenate(
            [
                lax.ppermute(tail, axis, [(i, (i + 1) % count) for i in range(ends)]),
                cells,
                lax.ppermute(head, axis, [((i + 1) % count, i) for i in range(ends)]),
            ],
            axis=dim,
        )
    return cells


def normalize(latent, gn_gain, gn_bias):
    values = latent.astype(jnp.float32)
    n_frames, n_rows, n_cols, n_chans = latent.shape
    group_ch = CH // GROUPS
    local_groups = n_chans // group_ch
    shaped = values.reshape(n_frames, n_rows, n_cols, local_groups, group_ch)
    part_sum = jnp.sum(shaped, axis=(0, 1, 2, 4))
    part_square = jnp.sum(shaped * shaped, axis=(0, 1, 2, 4))
    total_sum, total_square = lax.psum((part_sum, part_square), ("tm", "tile"))
    entries = n_frames * n_rows * n_cols * group_ch * lax.axis_size("tm") * lax.axis_size("tile")
    mean_grp = total_sum / entries
    square_grp = total_square / entries
    inv_grp = lax.rsqrt(square_grp - mean_grp * mean_grp + 1e-06)
    mean_ch = jnp.repeat(mean_grp, group_ch)
    inv_ch = jnp.repeat(inv_grp, group_ch)
    scaled = (values - mean_ch) * inv_ch * gn_gain.astype(jnp.float32) + gn_bias.astype(jnp.float32)
    return jax.nn.silu(scaled).astype(jnp.bfloat16)


def conv_term(padded, n_frames, n_rows, n_cols, block_in):
    width_in = block_in.shape[1]
    columns = [
        padded[
            time_off : time_off + n_frames, row_off : row_off + n_rows, col_off : col_off + n_cols
        ]
        for time_off in range(3)
        for row_off in range(3)
        for col_off in range(3)
    ]
    stacked = jnp.stack(columns, axis=3).reshape(n_frames * n_rows * n_cols, 27 * width_in)
    matrix = block_in.reshape(27 * width_in, block_in.shape[2])
    return jnp.dot(stacked, matrix, preferred_element_type=jnp.float32)


def body(latent, gn_gain, gn_bias, conv_weight, conv_bias):
    n_frames, n_rows, n_cols, n_chans = latent.shape
    normed = normalize(latent, gn_gain, gn_bias)
    full_feat = lax.all_gather(normed, "chan", axis=3, tiled=True)
    earlier = shifted(full_feat, "tm", 1)
    extended = jnp.concatenate([earlier, full_feat], axis=0)
    rimmed = extended_2(extended, (("tile", 2),), 1)
    padded = jnp.pad(rimmed, ((0, 0), (1, 1), (0, 0), (0, 0)))
    summed = conv_term(
        padded, n_frames, n_rows, n_cols, lax.all_gather(conv_weight, "tm", axis=1, tiled=True)
    )
    result = (summed + conv_bias.astype(jnp.float32)).astype(jnp.bfloat16)
    return result.reshape(n_frames, n_rows, n_cols, n_chans)


def near_of(s):
    return s + 1 - 2 * (s % 2)


def mid_of(s):
    return (s + 2) % 4


def far_of(s):
    return 3 - s


def edges_kernel(latent_ref, out_ref, wide_ref, *, cells, cols):
    wide = latent_ref[...].astype(jnp.float32)
    edges = cells // cols
    first = jnp.where(lax.axis_index("tile") == 0, cols - 1, 0)
    for k in range(wide.shape[1] // LANES):
        lanes = slice(k * LANES, (k + 1) * LANES)
        wide_ref[...] = wide[:, lanes]
        out_ref[:edges, lanes] = wide_ref[pl.ds(first, edges, stride=cols), :]
    total = jnp.sum(wide, axis=0, keepdims=True)
    square = jnp.sum(wide * wide, axis=0, keepdims=True)
    out_ref[edges:] = jnp.concatenate([total, square, jnp.zeros((6, wide.shape[1]), jnp.float32)], axis=0)


def three(value):
    high = value.astype(jnp.bfloat16)
    rest = value - high.astype(jnp.float32)
    mid = rest.astype(jnp.bfloat16)
    low = (rest - mid.astype(jnp.float32)).astype(jnp.bfloat16)
    return [high, mid, low]


def pack_kernel(latent_ref, own_ref, other_ref, gain_ref, bias_ref, same_ref, next_ref, *, cells, edges):
    sums = own_ref[edges : edges + 2] + other_ref[edges : edges + 2]
    tail = three(sums[0:1]) + three(sums[1:2]) + [gain_ref[...], bias_ref[...]]
    tail = jnp.concatenate([row.astype(jnp.float32) for row in tail], axis=0)
    tail = jnp.concatenate([tail, jnp.zeros_like(tail)], axis=0).astype(jnp.bfloat16)
    edge = other_ref[:edges].astype(jnp.bfloat16)

    def fill(out_ref, block):
        lanes = slice(block * LANES, (block + 1) * LANES)
        out_ref[:cells] = latent_ref[:, lanes]
        out_ref[cells : cells + edges] = edge[:, lanes]
        out_ref[cells + edges :] = tail[:, lanes]

    parity = lax.axis_index("tm") % 2

    @pl.when(parity == 0)
    def _():
        fill(same_ref, 0)
        fill(next_ref, 1)

    @pl.when(parity == 1)
    def _():
        fill(same_ref, 1)
        fill(next_ref, 0)


def group_total(row, group_ch):
    lane = lax.broadcasted_iota(jnp.int32, row.shape, 1)
    step = 1
    while step < group_ch:
        up = pltpu.roll(row, LANES - step, 1)
        down = pltpu.roll(row, step, 1)
        row = row + jnp.where((lane // step) % 2 == 0, up, down)
        step *= 2
    return row


def spread_kernel(same_ref, a_ref, b_ref, c_ref, d_ref, out_ref, own_ref, *, frames, rows, cols, entries):
    s = lax.axis_index("tm")
    home = lax.axis_index("chan") == s // 2
    tile = lax.axis_index("tile")
    cells = frames * rows * cols
    edges = frames * rows
    base = cells + edges

    @pl.when(home)
    def _():
        own_ref[...] = same_ref[...]

    @pl.when(jnp.logical_not(home))
    def _():
        own_ref[...] = d_ref[...]

    near, mid, far = near_of(s), mid_of(s), far_of(s)
    pieces = (
        (own_ref, jnp.where(home, s, mid)),
        (a_ref, jnp.where(home, near, far)),
        (b_ref, jnp.where(home, mid, s)),
        (c_ref, jnp.where(home, far, near)),
    )
    tails = [ref[base : base + STAT_ROWS].astype(jnp.float32) for ref, _ in pieces]
    stats = tails[0] + tails[1] + tails[2] + tails[3]
    total = group_total(stats[0:1] + stats[1:2] + stats[2:3], CH // GROUPS) / entries
    square = group_total(stats[3:4] + stats[4:5] + stats[5:6], CH // GROUPS) / entries
    scale = lax.rsqrt(square - total * total + EPS) * tails[0][6:7]
    shift = tails[0][7:8]

    def normed(raw):
        value = (raw.astype(jnp.float32) - total) * scale + shift
        return value / (1.0 + jnp.exp(-value))

    n_all = out_ref.shape[1]
    zero_row = jnp.zeros((cols, LANES), jnp.bfloat16)
    for d in range(3):
        for f in range(n_all):
            out_ref[d, f, 0] = zero_row
            out_ref[d, f, rows + 1] = zero_row
        for f in range(2):
            out_ref[d, f, 1 : rows + 1] = jnp.zeros((rows, cols, LANES), jnp.bfloat16)
    col = lax.broadcasted_iota(jnp.int32, (rows, cols, LANES), 1)
    span = rows * cols
    for ref, block in pieces:
        for f in range(frames):
            value = normed(ref[f * span : (f + 1) * span])
            edge = normed(ref[cells + f * rows : cells + (f + 1) * rows])
            edge = jnp.broadcast_to(edge[:, None, :], (rows, cols, LANES))
            left = pltpu.roll(value, 1, 0).reshape(rows, cols, LANES)
            left = jnp.where(col == 0, jnp.where(tile == 1, edge, 0.0), left)
            right = pltpu.roll(value, span - 1, 0).reshape(rows, cols, LANES)
            right = jnp.where(col == cols - 1, jnp.where(tile == 0, edge, 0.0), right)
            at = 2 + block * frames + f
            out_ref[0, at, 1 : rows + 1] = left.astype(jnp.bfloat16)
            out_ref[1, at, 1 : rows + 1] = value.reshape(rows, cols, LANES).astype(jnp.bfloat16)
            out_ref[2, at, 1 : rows + 1] = right.astype(jnp.bfloat16)


def partial_kernel(spread_ref, weight_ref, *rest, block_of, frame_list, frames, rows, cols, adds, with_bias):
    out_ref = rest[-1]
    block = block_of(lax.axis_index("tm"))
    span = rows * cols
    for k, f in enumerate(frame_list):
        at = block * frames + f
        stacked = jnp.concatenate(
            [
                spread_ref[d, at + a, b : b + rows].reshape(span, LANES)
                for a in range(3)
                for b in range(3)
                for d in range(3)
            ],
            axis=1,
        )
        total = jnp.dot(stacked, weight_ref[...], preferred_element_type=jnp.float32)
        for ref, frame in zip(rest, adds):
            if frame == f:
                total = total + ref[...].astype(jnp.float32)
        if with_bias:
            total = total + rest[len(adds)][...].astype(jnp.float32)
        out_ref[k * span : (k + 1) * span] = total.astype(out_ref.dtype)


def finish_kernel(home_ref, beside_ref, *rest, span):
    out_ref = rest[-1]
    total = home_ref[...] + beside_ref[...].astype(jnp.float32)
    out_ref[:span] = total[:span].astype(out_ref.dtype)
    for k, ref in enumerate(rest[:-1]):
        here = slice((k + 1) * span, (k + 2) * span)
        out_ref[here] = (total[here] + ref[...].astype(jnp.float32)).astype(out_ref.dtype)


def params():
    return pltpu.CompilerParams(vmem_limit_bytes=VMEM)


def split_body(latent, gn_gain, gn_bias, conv_weight, conv_bias):
    frames, rows, cols, chans = latent.shape
    outs = conv_weight.shape[2]
    cells = frames * rows * cols
    edges = frames * rows
    n_blocks = lax.axis_size("tm")
    entries = cells * n_blocks * lax.axis_size("tile") * (CH // GROUPS)
    flat = latent.reshape(cells, chans)

    own = pl.pallas_call(
        functools.partial(edges_kernel, cells=cells, cols=cols),
        out_shape=jax.ShapeDtypeStruct((edges + 8, chans), jnp.float32),
        scratch_shapes=[pltpu.VMEM((cells, LANES), jnp.float32)],
        compiler_params=params(),
    )(flat)
    other = lax.ppermute(own, "tile", [(0, 1), (1, 0)])
    packed = jax.ShapeDtypeStruct((cells + edges + STAT_ROWS, LANES), jnp.bfloat16)
    same, following = pl.pallas_call(
        functools.partial(pack_kernel, cells=cells, edges=edges),
        out_shape=(packed, packed),
        compiler_params=params(),
    )(flat, own, other, gn_gain.reshape(1, chans), gn_bias.reshape(1, chans))

    both = ("tm", "chan")
    route_a, route_b, route_d = [], [], []
    for s in range(n_blocks):
        h = s // 2
        route_a += [(2 * s + h, 2 * near_of(s) + h), (2 * s + 1 - h, 2 * far_of(s) + h)]
        route_b += [(2 * s + h, 2 * s + 1 - h), (2 * s + 1 - h, 2 * mid_of(s) + 1 - h)]
        route_d += [(2 * s + h, 2 * s + 1 - h)]
    got_a = lax.ppermute(following, both, route_a)
    got_b = lax.ppermute(same, both, route_b)
    got_c = lax.ppermute(got_a, "chan", [(0, 1), (1, 0)])
    got_d = lax.ppermute(got_b, both, route_d)
    spread = pl.pallas_call(
        functools.partial(spread_kernel, frames=frames, rows=rows, cols=cols, entries=entries),
        out_shape=jax.ShapeDtypeStruct((3, n_blocks * frames + 2, rows + 2, cols, LANES), jnp.bfloat16),
        scratch_shapes=[pltpu.VMEM(packed.shape, jnp.bfloat16)],
        compiler_params=params(),
    )(same, got_a, got_b, got_c, got_d)

    weight = conv_weight.reshape(27 * LANES, outs)
    bias = conv_bias.reshape(1, outs)

    every = tuple(range(frames))

    def partial_sum(block_of, frame_list=every, adds=(), with_bias=False, dtype=jnp.bfloat16, after=None, cost=1):
        source = spread if after is None else lax.optimization_barrier((spread, after))[0]
        size = len(frame_list) * rows * cols
        return pl.pallas_call(
            functools.partial(
                partial_kernel,
                block_of=block_of,
                frame_list=frame_list,
                frames=frames,
                rows=rows,
                cols=cols,
                adds=frame_list[: len(adds)],
                with_bias=with_bias,
            ),
            out_shape=jax.ShapeDtypeStruct((size, outs), dtype),
            compiler_params=params(),
            cost_estimate=pl.CostEstimate(flops=cost, transcendentals=0, bytes_accessed=1),
        )(source, weight, *adds, *([bias] if with_bias else []))

    near_route = [(s, near_of(s)) for s in range(n_blocks)]
    far_route = [(s, far_of(s)) for s in range(n_blocks)]
    parts = []
    for f in every:
        parts.append(partial_sum(lambda s: far_of(near_of(s)), (f,), after=parts[-1] if parts else None, cost=1 << 32))
    beyond = [lax.ppermute(part, "tm", near_route) for part in parts]
    sums = [partial_sum(far_of, (f,), (beyond[f],)) for f in every]
    arrived = [lax.ppermute(part, "tm", far_route) for part in sums]
    beside = lax.ppermute(partial_sum(near_of, after=(sums[0], beyond[-1])), "tm", near_route)
    home = partial_sum(lambda s: s, every, arrived[:1], True, jnp.float32, cost=1 << 35)
    result = pl.pallas_call(
        functools.partial(finish_kernel, span=rows * cols),
        out_shape=jax.ShapeDtypeStruct((cells, outs), jnp.bfloat16),
        compiler_params=params(),
    )(home, beside, *arrived[1:])
    return result.reshape(frames, rows, cols, outs)


def splits(mesh):
    size = mesh.shape
    return size["tm"] == 4 and size["tile"] == 2 and size["chan"] == 2 and CH == size["tm"] * LANES


def solution(mesh):
    in_specs = (
        P(("groups", "tm"), None, "tile", "chan"),
        P("chan"),
        P("chan"),
        P(None, "tm", "chan"),
        P("chan"),
    )
    out_specs = P(("groups", "tm"), None, "tile", "chan")
    chosen = split_body if splits(mesh) else body
    return jax.shard_map(chosen, mesh=mesh, in_specs=in_specs, out_specs=out_specs, check_vma=False)
```

```python
import functools

import jax
import jax.numpy as jnp
from jax import lax
from jax.experimental import pallas as pl
from jax.experimental.pallas import tpu as pltpu
from jax.sharding import PartitionSpec as P

CH = 512
GROUPS = 32
EPS = 1e-06
LANES = 128
VMEM = 24 << 20
STAT_ROWS = 16


def shifted(block, axis, distance):
    devices = range(lax.axis_size(axis))
    route = [(i - distance, i) for i in devices if i - distance in devices]
    return lax.ppermute(block, axis, route)


def extended_2(cells, sides, width):
    for axis, dim in sides:
        count = lax.axis_size(axis)
        ends = count - 1
        head = lax.slice_in_dim(cells, 0, width, axis=dim)
        tail = lax.slice_in_dim(cells, cells.shape[dim] - width, cells.shape[dim], axis=dim)
        cells = jnp.concatenate(
            [
                lax.ppermute(tail, axis, [(i, (i + 1) % count) for i in range(ends)]),
                cells,
                lax.ppermute(head, axis, [((i + 1) % count, i) for i in range(ends)]),
            ],
            axis=dim,
        )
    return cells


def normalize(latent, gn_gain, gn_bias):
    values = latent.astype(jnp.float32)
    n_frames, n_rows, n_cols, n_chans = latent.shape
    group_ch = CH // GROUPS
    local_groups = n_chans // group_ch
    shaped = values.reshape(n_frames, n_rows, n_cols, local_groups, group_ch)
    part_sum = jnp.sum(shaped, axis=(0, 1, 2, 4))
    part_square = jnp.sum(shaped * shaped, axis=(0, 1, 2, 4))
    total_sum, total_square = lax.psum((part_sum, part_square), ("tm", "tile"))
    entries = n_frames * n_rows * n_cols * group_ch * lax.axis_size("tm") * lax.axis_size("tile")
    mean_grp = total_sum / entries
    square_grp = total_square / entries
    inv_grp = lax.rsqrt(square_grp - mean_grp * mean_grp + 1e-06)
    mean_ch = jnp.repeat(mean_grp, group_ch)
    inv_ch = jnp.repeat(inv_grp, group_ch)
    scaled = (values - mean_ch) * inv_ch * gn_gain.astype(jnp.float32) + gn_bias.astype(jnp.float32)
    return jax.nn.silu(scaled).astype(jnp.bfloat16)


def conv_term(padded, n_frames, n_rows, n_cols, block_in):
    width_in = block_in.shape[1]
    columns = [
        padded[
            time_off : time_off + n_frames, row_off : row_off + n_rows, col_off : col_off + n_cols
        ]
        for time_off in range(3)
        for row_off in range(3)
        for col_off in range(3)
    ]
    stacked = jnp.stack(columns, axis=3).reshape(n_frames * n_rows * n_cols, 27 * width_in)
    matrix = block_in.reshape(27 * width_in, block_in.shape[2])
    return jnp.dot(stacked, matrix, preferred_element_type=jnp.float32)


def body(latent, gn_gain, gn_bias, conv_weight, conv_bias):
    n_frames, n_rows, n_cols, n_chans = latent.shape
    normed = normalize(latent, gn_gain, gn_bias)
    full_feat = lax.all_gather(normed, "chan", axis=3, tiled=True)
    earlier = shifted(full_feat, "tm", 1)
    extended = jnp.concatenate([earlier, full_feat], axis=0)
    rimmed = extended_2(extended, (("tile", 2),), 1)
    padded = jnp.pad(rimmed, ((0, 0), (1, 1), (0, 0), (0, 0)))
    summed = conv_term(
        padded, n_frames, n_rows, n_cols, lax.all_gather(conv_weight, "tm", axis=1, tiled=True)
    )
    result = (summed + conv_bias.astype(jnp.float32)).astype(jnp.bfloat16)
    return result.reshape(n_frames, n_rows, n_cols, n_chans)


def near_of(s):
    return s + 1 - 2 * (s % 2)


def mid_of(s):
    return (s + 2) % 4


def far_of(s):
    return 3 - s


def edges_kernel(latent_ref, out_ref, wide_ref, *, cells, cols):
    wide = latent_ref[...].astype(jnp.float32)
    edges = cells // cols
    first = jnp.where(lax.axis_index("tile") == 0, cols - 1, 0)
    for k in range(wide.shape[1] // LANES):
        lanes = slice(k * LANES, (k + 1) * LANES)
        wide_ref[...] = wide[:, lanes]
        out_ref[:edges, lanes] = wide_ref[pl.ds(first, edges, stride=cols), :]
    total = jnp.sum(wide, axis=0, keepdims=True)
    square = jnp.sum(wide * wide, axis=0, keepdims=True)
    out_ref[edges:] = jnp.concatenate([total, square, jnp.zeros((6, wide.shape[1]), jnp.float32)], axis=0)


def three(value):
    high = value.astype(jnp.bfloat16)
    rest = value - high.astype(jnp.float32)
    mid = rest.astype(jnp.bfloat16)
    low = (rest - mid.astype(jnp.float32)).astype(jnp.bfloat16)
    return [high, mid, low]


def pack_kernel(latent_ref, own_ref, other_ref, gain_ref, bias_ref, same_ref, next_ref, *, cells, edges):
    sums = own_ref[edges : edges + 2] + other_ref[edges : edges + 2]
    tail = three(sums[0:1]) + three(sums[1:2]) + [gain_ref[...], bias_ref[...]]
    tail = jnp.concatenate([row.astype(jnp.float32) for row in tail], axis=0)
    tail = jnp.concatenate([tail, jnp.zeros_like(tail)], axis=0).astype(jnp.bfloat16)
    edge = other_ref[:edges].astype(jnp.bfloat16)

    def fill(out_ref, block):
        lanes = slice(block * LANES, (block + 1) * LANES)
        out_ref[:cells] = latent_ref[:, lanes]
        out_ref[cells : cells + edges] = edge[:, lanes]
        out_ref[cells + edges :] = tail[:, lanes]

    parity = lax.axis_index("tm") % 2

    @pl.when(parity == 0)
    def _():
        fill(same_ref, 0)
        fill(next_ref, 1)

    @pl.when(parity == 1)
    def _():
        fill(same_ref, 1)
        fill(next_ref, 0)


def group_total(row, group_ch):
    lane = lax.broadcasted_iota(jnp.int32, row.shape, 1)
    step = 1
    while step < group_ch:
        up = pltpu.roll(row, LANES - step, 1)
        down = pltpu.roll(row, step, 1)
        row = row + jnp.where((lane // step) % 2 == 0, up, down)
        step *= 2
    return row


def spread_kernel(same_ref, a_ref, b_ref, c_ref, d_ref, out_ref, own_ref, *, frames, rows, cols, entries):
    s = lax.axis_index("tm")
    home = lax.axis_index("chan") == s // 2
    tile = lax.axis_index("tile")
    cells = frames * rows * cols
    edges = frames * rows
    base = cells + edges

    @pl.when(home)
    def _():
        own_ref[...] = same_ref[...]

    @pl.when(jnp.logical_not(home))
    def _():
        own_ref[...] = d_ref[...]

    near, mid, far = near_of(s), mid_of(s), far_of(s)
    pieces = (
        (own_ref, jnp.where(home, s, mid)),
        (a_ref, jnp.where(home, near, far)),
        (b_ref, jnp.where(home, mid, s)),
        (c_ref, jnp.where(home, far, near)),
    )
    tails = [ref[base : base + STAT_ROWS].astype(jnp.float32) for ref, _ in pieces]
    stats = tails[0] + tails[1] + tails[2] + tails[3]
    total = group_total(stats[0:1] + stats[1:2] + stats[2:3], CH // GROUPS) / entries
    square = group_total(stats[3:4] + stats[4:5] + stats[5:6], CH // GROUPS) / entries
    scale = lax.rsqrt(square - total * total + EPS) * tails[0][6:7]
    shift = tails[0][7:8]

    def normed(raw):
        value = (raw.astype(jnp.float32) - total) * scale + shift
        return value / (1.0 + jnp.exp(-value))

    n_all = out_ref.shape[1]
    zero_row = jnp.zeros((cols, LANES), jnp.bfloat16)
    for d in range(3):
        for f in range(n_all):
            out_ref[d, f, 0] = zero_row
            out_ref[d, f, rows + 1] = zero_row
        for f in range(2):
            out_ref[d, f, 1 : rows + 1] = jnp.zeros((rows, cols, LANES), jnp.bfloat16)
    col = lax.broadcasted_iota(jnp.int32, (rows, cols, LANES), 1)
    span = rows * cols
    for ref, block in pieces:
        for f in range(frames):
            value = normed(ref[f * span : (f + 1) * span])
            edge = normed(ref[cells + f * rows : cells + (f + 1) * rows])
            edge = jnp.broadcast_to(edge[:, None, :], (rows, cols, LANES))
            left = pltpu.roll(value, 1, 0).reshape(rows, cols, LANES)
            left = jnp.where(col == 0, jnp.where(tile == 1, edge, 0.0), left)
            right = pltpu.roll(value, span - 1, 0).reshape(rows, cols, LANES)
            right = jnp.where(col == cols - 1, jnp.where(tile == 0, edge, 0.0), right)
            at = 2 + block * frames + f
            out_ref[0, at, 1 : rows + 1] = left.astype(jnp.bfloat16)
            out_ref[1, at, 1 : rows + 1] = value.reshape(rows, cols, LANES).astype(jnp.bfloat16)
            out_ref[2, at, 1 : rows + 1] = right.astype(jnp.bfloat16)


def partial_kernel(spread_ref, weight_ref, *rest, jobs, n_adds, n_outs, frames, rows, cols, with_bias):
    outs = rest[len(rest) - n_outs :]
    s = lax.axis_index("tm")
    span = rows * cols
    for block_of, f, out, place, added in jobs:
        at = block_of(s) * frames + f
        stacked = jnp.concatenate(
            [
                spread_ref[d, at + a, b : b + rows].reshape(span, LANES)
                for a in range(3)
                for b in range(3)
                for d in range(3)
            ],
            axis=1,
        )
        total = jnp.dot(stacked, weight_ref[...], preferred_element_type=jnp.float32)
        if added is not None:
            total = total + rest[added][...].astype(jnp.float32)
        if with_bias:
            total = total + rest[n_adds][...].astype(jnp.float32)
        outs[out][place * span : (place + 1) * span] = total.astype(outs[out].dtype)


def finish_kernel(home_ref, beside_ref, *rest, span):
    out_ref = rest[-1]
    total = home_ref[...] + beside_ref[...].astype(jnp.float32)
    out_ref[:span] = total[:span].astype(out_ref.dtype)
    for k, ref in enumerate(rest[:-1]):
        here = slice((k + 1) * span, (k + 2) * span)
        out_ref[here] = (total[here] + ref[...].astype(jnp.float32)).astype(out_ref.dtype)


def params():
    return pltpu.CompilerParams(vmem_limit_bytes=VMEM)


def split_body(latent, gn_gain, gn_bias, conv_weight, conv_bias):
    frames, rows, cols, chans = latent.shape
    outs = conv_weight.shape[2]
    cells = frames * rows * cols
    edges = frames * rows
    n_blocks = lax.axis_size("tm")
    entries = cells * n_blocks * lax.axis_size("tile") * (CH // GROUPS)
    flat = latent.reshape(cells, chans)

    own = pl.pallas_call(
        functools.partial(edges_kernel, cells=cells, cols=cols),
        out_shape=jax.ShapeDtypeStruct((edges + 8, chans), jnp.float32),
        scratch_shapes=[pltpu.VMEM((cells, LANES), jnp.float32)],
        compiler_params=params(),
    )(flat)
    other = lax.ppermute(own, "tile", [(0, 1), (1, 0)])
    packed = jax.ShapeDtypeStruct((cells + edges + STAT_ROWS, LANES), jnp.bfloat16)
    same, following = pl.pallas_call(
        functools.partial(pack_kernel, cells=cells, edges=edges),
        out_shape=(packed, packed),
        compiler_params=params(),
    )(flat, own, other, gn_gain.reshape(1, chans), gn_bias.reshape(1, chans))

    both = ("tm", "chan")
    route_a, route_b, route_d = [], [], []
    for s in range(n_blocks):
        h = s // 2
        route_a += [(2 * s + h, 2 * near_of(s) + h), (2 * s + 1 - h, 2 * far_of(s) + h)]
        route_b += [(2 * s + h, 2 * s + 1 - h), (2 * s + 1 - h, 2 * mid_of(s) + 1 - h)]
        route_d += [(2 * s + h, 2 * s + 1 - h)]
    got_a = lax.ppermute(following, both, route_a)
    got_b = lax.ppermute(same, both, route_b)
    got_c = lax.ppermute(got_a, "chan", [(0, 1), (1, 0)])
    got_d = lax.ppermute(got_b, both, route_d)
    spread = pl.pallas_call(
        functools.partial(spread_kernel, frames=frames, rows=rows, cols=cols, entries=entries),
        out_shape=jax.ShapeDtypeStruct((3, n_blocks * frames + 2, rows + 2, cols, LANES), jnp.bfloat16),
        scratch_shapes=[pltpu.VMEM(packed.shape, jnp.bfloat16)],
        compiler_params=params(),
    )(same, got_a, got_b, got_c, got_d)

    weight = conv_weight.reshape(27 * LANES, outs)
    bias = conv_bias.reshape(1, outs)

    every = tuple(range(frames))

    def partial_sums(jobs, spans, adds=(), with_bias=False, dtype=jnp.bfloat16, after=None, cost=1):
        source = spread if after is None else lax.optimization_barrier((spread, after))[0]
        return pl.pallas_call(
            functools.partial(
                partial_kernel,
                jobs=jobs,
                n_adds=len(adds),
                n_outs=len(spans),
                frames=frames,
                rows=rows,
                cols=cols,
                with_bias=with_bias,
            ),
            out_shape=[jax.ShapeDtypeStruct((n * rows * cols, outs), dtype) for n in spans],
            compiler_params=params(),
            cost_estimate=pl.CostEstimate(flops=cost, transcendentals=0, bytes_accessed=1),
        )(source, weight, *adds, *([bias] if with_bias else []))

    def beyond_of(s):
        return far_of(near_of(s))

    near_route = [(s, near_of(s)) for s in range(n_blocks)]
    far_route = [(s, far_of(s)) for s in range(n_blocks)]
    parts = []
    for f in every:
        jobs, spans = [(beyond_of, f, 0, 0, None)], [1]
        if f == frames - 1:
            jobs += [(near_of, g, 1, g, None) for g in every]
            spans += [frames]
        parts.append(partial_sums(jobs, spans, after=parts[-1] if parts else None, cost=1 << 32))
    beyond = [lax.ppermute(part[0], "tm", near_route) for part in parts]
    sums = [partial_sums([(far_of, f, 0, 0, 0)], [1], (beyond[f],))[0] for f in every]
    arrived = [lax.ppermute(part, "tm", far_route) for part in sums]
    beside = lax.ppermute(parts[-1][1], "tm", near_route)
    home = partial_sums(
        [(lambda s: s, f, 0, f, None if f else 0) for f in every],
        [frames],
        arrived[:1],
        True,
        jnp.float32,
        cost=1 << 35,
    )[0]
    result = pl.pallas_call(
        functools.partial(finish_kernel, span=rows * cols),
        out_shape=jax.ShapeDtypeStruct((cells, outs), jnp.bfloat16),
        compiler_params=params(),
    )(home, beside, *arrived[1:])
    return result.reshape(frames, rows, cols, outs)


def splits(mesh):
    size = mesh.shape
    return size["tm"] == 4 and size["tile"] == 2 and size["chan"] == 2 and CH == size["tm"] * LANES


def solution(mesh):
    in_specs = (
        P(("groups", "tm"), None, "tile", "chan"),
        P("chan"),
        P("chan"),
        P(None, "tm", "chan"),
        P("chan"),
    )
    out_specs = P(("groups", "tm"), None, "tile", "chan")
    chosen = split_body if splits(mesh) else body
    return jax.shard_map(chosen, mesh=mesh, in_specs=in_specs, out_specs=out_specs, check_vma=False)
```

```python
import functools

import jax
import jax.numpy as jnp
from jax import lax
from jax.experimental import pallas as pl
from jax.experimental.pallas import tpu as pltpu
from jax.sharding import PartitionSpec as P

CH = 512
GROUPS = 32
EPS = 1e-06
LANES = 128
VMEM = 24 << 20
STAT_ROWS = 16


def shifted(block, axis, distance):
    devices = range(lax.axis_size(axis))
    route = [(i - distance, i) for i in devices if i - distance in devices]
    return lax.ppermute(block, axis, route)


def extended_2(cells, sides, width):
    for axis, dim in sides:
        count = lax.axis_size(axis)
        ends = count - 1
        head = lax.slice_in_dim(cells, 0, width, axis=dim)
        tail = lax.slice_in_dim(cells, cells.shape[dim] - width, cells.shape[dim], axis=dim)
        cells = jnp.concatenate(
            [
                lax.ppermute(tail, axis, [(i, (i + 1) % count) for i in range(ends)]),
                cells,
                lax.ppermute(head, axis, [((i + 1) % count, i) for i in range(ends)]),
            ],
            axis=dim,
        )
    return cells


def normalize(latent, gn_gain, gn_bias):
    values = latent.astype(jnp.float32)
    n_frames, n_rows, n_cols, n_chans = latent.shape
    group_ch = CH // GROUPS
    local_groups = n_chans // group_ch
    shaped = values.reshape(n_frames, n_rows, n_cols, local_groups, group_ch)
    part_sum = jnp.sum(shaped, axis=(0, 1, 2, 4))
    part_square = jnp.sum(shaped * shaped, axis=(0, 1, 2, 4))
    total_sum, total_square = lax.psum((part_sum, part_square), ("tm", "tile"))
    entries = n_frames * n_rows * n_cols * group_ch * lax.axis_size("tm") * lax.axis_size("tile")
    mean_grp = total_sum / entries
    square_grp = total_square / entries
    inv_grp = lax.rsqrt(square_grp - mean_grp * mean_grp + 1e-06)
    mean_ch = jnp.repeat(mean_grp, group_ch)
    inv_ch = jnp.repeat(inv_grp, group_ch)
    scaled = (values - mean_ch) * inv_ch * gn_gain.astype(jnp.float32) + gn_bias.astype(jnp.float32)
    return jax.nn.silu(scaled).astype(jnp.bfloat16)


def conv_term(padded, n_frames, n_rows, n_cols, block_in):
    width_in = block_in.shape[1]
    columns = [
        padded[
            time_off : time_off + n_frames, row_off : row_off + n_rows, col_off : col_off + n_cols
        ]
        for time_off in range(3)
        for row_off in range(3)
        for col_off in range(3)
    ]
    stacked = jnp.stack(columns, axis=3).reshape(n_frames * n_rows * n_cols, 27 * width_in)
    matrix = block_in.reshape(27 * width_in, block_in.shape[2])
    return jnp.dot(stacked, matrix, preferred_element_type=jnp.float32)


def body(latent, gn_gain, gn_bias, conv_weight, conv_bias):
    n_frames, n_rows, n_cols, n_chans = latent.shape
    normed = normalize(latent, gn_gain, gn_bias)
    full_feat = lax.all_gather(normed, "chan", axis=3, tiled=True)
    earlier = shifted(full_feat, "tm", 1)
    extended = jnp.concatenate([earlier, full_feat], axis=0)
    rimmed = extended_2(extended, (("tile", 2),), 1)
    padded = jnp.pad(rimmed, ((0, 0), (1, 1), (0, 0), (0, 0)))
    summed = conv_term(
        padded, n_frames, n_rows, n_cols, lax.all_gather(conv_weight, "tm", axis=1, tiled=True)
    )
    result = (summed + conv_bias.astype(jnp.float32)).astype(jnp.bfloat16)
    return result.reshape(n_frames, n_rows, n_cols, n_chans)


def near_of(s):
    return s + 1 - 2 * (s % 2)


def mid_of(s):
    return (s + 2) % 4


def far_of(s):
    return 3 - s


def three(value):
    high = value.astype(jnp.bfloat16)
    rest = value - high.astype(jnp.float32)
    mid = rest.astype(jnp.bfloat16)
    low = (rest - mid.astype(jnp.float32)).astype(jnp.bfloat16)
    return [high.astype(jnp.float32), mid.astype(jnp.float32), low.astype(jnp.float32)]


def tail_rows(rows):
    rows = jnp.concatenate(rows, axis=0)
    filler = jnp.zeros((STAT_ROWS - rows.shape[0], rows.shape[1]), jnp.float32)
    return jnp.concatenate([rows, filler], axis=0).astype(jnp.bfloat16)


def sum_rows(wide):
    total = jnp.sum(wide, axis=0, keepdims=True)
    square = jnp.sum(wide * wide, axis=0, keepdims=True)
    return three(total) + three(square)


def by_parity(fill):
    parity = lax.axis_index("tm") % 2

    @pl.when(parity == 0)
    def _():
        fill(slice(0, LANES), slice(LANES, 2 * LANES))

    @pl.when(parity == 1)
    def _():
        fill(slice(LANES, 2 * LANES), slice(0, LANES))


def cells_kernel(latent_ref, same_ref, next_ref, *, cells):
    def fill(same, following):
        for out_ref, lanes in ((same_ref, same), (next_ref, following)):
            out_ref[:cells] = latent_ref[:, lanes]
            out_ref[cells:] = tail_rows(sum_rows(latent_ref[:, lanes].astype(jnp.float32)))

    by_parity(fill)


def edges_kernel(latent_ref, gain_ref, bias_ref, same_ref, next_ref, wide_ref, *, edges, cols):
    first = jnp.where(lax.axis_index("tile") == 0, cols - 1, 0)

    def fill(same, following):
        for out_ref, lanes in ((same_ref, same), (next_ref, following)):
            wide = latent_ref[:, lanes].astype(jnp.float32)
            wide_ref[...] = wide
            out_ref[:edges] = wide_ref[pl.ds(first, edges, stride=cols), :].astype(jnp.bfloat16)
            params_rows = [ref[:, lanes].astype(jnp.float32) for ref in (gain_ref, bias_ref)]
            out_ref[edges:] = tail_rows(sum_rows(wide) + params_rows)

    by_parity(fill)


def join_kernel(first_ref, second_ref, out_ref):
    split = first_ref.shape[0]
    out_ref[:split] = first_ref[...]
    out_ref[split:] = second_ref[...]


def group_total(row, group_ch):
    lane = lax.broadcasted_iota(jnp.int32, row.shape, 1)
    step = 1
    while step < group_ch:
        up = pltpu.roll(row, LANES - step, 1)
        down = pltpu.roll(row, step, 1)
        row = row + jnp.where((lane // step) % 2 == 0, up, down)
        step *= 2
    return row


def spread_kernel(
    same_ref, a_ref, edge_a_ref, b_ref, edge_b_ref, c_ref, d_ref, out_ref, own_ref, *, frames, rows, cols, entries
):
    s = lax.axis_index("tm")
    home = lax.axis_index("chan") == s // 2
    tile = lax.axis_index("tile")
    cells = frames * rows * cols
    edges = frames * rows
    split = cells + STAT_ROWS

    @pl.when(home)
    def _():
        own_ref[...] = same_ref[...]

    @pl.when(jnp.logical_not(home))
    def _():
        own_ref[...] = d_ref[:split]

    near, mid, far = near_of(s), mid_of(s), far_of(s)
    pieces = (
        (own_ref, d_ref, split, jnp.where(home, s, mid)),
        (a_ref, edge_a_ref, 0, jnp.where(home, near, far)),
        (b_ref, edge_b_ref, 0, jnp.where(home, mid, s)),
        (c_ref, c_ref, split, jnp.where(home, far, near)),
    )
    stats = jnp.zeros((STAT_ROWS, LANES), jnp.float32)
    for ref, edge_ref, skip, _ in pieces:
        last = edge_ref[skip + edges : skip + edges + STAT_ROWS].astype(jnp.float32)
        stats = stats + ref[cells : cells + STAT_ROWS].astype(jnp.float32) + last
    total = group_total(stats[0:1] + stats[1:2] + stats[2:3], CH // GROUPS) / entries
    square = group_total(stats[3:4] + stats[4:5] + stats[5:6], CH // GROUPS) / entries
    scale = lax.rsqrt(square - total * total + EPS) * last[6:7]
    shift = last[7:8]

    def normed(raw):
        value = (raw.astype(jnp.float32) - total) * scale + shift
        return value / (1.0 + jnp.exp(-value))

    n_all = out_ref.shape[1]
    zero_row = jnp.zeros((cols, LANES), jnp.bfloat16)
    for d in range(3):
        for f in range(n_all):
            out_ref[d, f, 0] = zero_row
            out_ref[d, f, rows + 1] = zero_row
        for f in range(2):
            out_ref[d, f, 1 : rows + 1] = jnp.zeros((rows, cols, LANES), jnp.bfloat16)
    col = lax.broadcasted_iota(jnp.int32, (rows, cols, LANES), 1)
    span = rows * cols
    for ref, edge_ref, skip, block in pieces:
        for f in range(frames):
            value = normed(ref[f * span : (f + 1) * span])
            edge = normed(edge_ref[skip + f * rows : skip + (f + 1) * rows])
            edge = jnp.broadcast_to(edge[:, None, :], (rows, cols, LANES))
            left = pltpu.roll(value, 1, 0).reshape(rows, cols, LANES)
            left = jnp.where(col == 0, jnp.where(tile == 1, edge, 0.0), left)
            right = pltpu.roll(value, span - 1, 0).reshape(rows, cols, LANES)
            right = jnp.where(col == cols - 1, jnp.where(tile == 0, edge, 0.0), right)
            at = 2 + block * frames + f
            out_ref[0, at, 1 : rows + 1] = left.astype(jnp.bfloat16)
            out_ref[1, at, 1 : rows + 1] = value.reshape(rows, cols, LANES).astype(jnp.bfloat16)
            out_ref[2, at, 1 : rows + 1] = right.astype(jnp.bfloat16)


def partial_kernel(spread_ref, weight_ref, *rest, jobs, n_adds, n_outs, frames, rows, cols, with_bias):
    outs = rest[len(rest) - n_outs :]
    s = lax.axis_index("tm")
    span = rows * cols
    for block_of, f, out, place, added in jobs:
        at = block_of(s) * frames + f
        stacked = jnp.concatenate(
            [
                spread_ref[d, at + a, b : b + rows].reshape(span, LANES)
                for a in range(3)
                for b in range(3)
                for d in range(3)
            ],
            axis=1,
        )
        total = jnp.dot(stacked, weight_ref[...], preferred_element_type=jnp.float32)
        if added is not None:
            total = total + rest[added][...].astype(jnp.float32)
        if with_bias:
            total = total + rest[n_adds][...].astype(jnp.float32)
        outs[out][place * span : (place + 1) * span] = total.astype(outs[out].dtype)


def finish_kernel(home_ref, beside_ref, *rest, span):
    out_ref = rest[-1]
    total = home_ref[...] + beside_ref[...].astype(jnp.float32)
    out_ref[:span] = total[:span].astype(out_ref.dtype)
    for k, ref in enumerate(rest[:-1]):
        here = slice((k + 1) * span, (k + 2) * span)
        out_ref[here] = (total[here] + ref[...].astype(jnp.float32)).astype(out_ref.dtype)


def params():
    return pltpu.CompilerParams(vmem_limit_bytes=VMEM)


def split_body(latent, gn_gain, gn_bias, conv_weight, conv_bias):
    frames, rows, cols, chans = latent.shape
    outs = conv_weight.shape[2]
    cells = frames * rows * cols
    edges = frames * rows
    n_blocks = lax.axis_size("tm")
    entries = cells * n_blocks * lax.axis_size("tile") * (CH // GROUPS)
    flat = latent.reshape(cells, chans)

    def table(height):
        return jax.ShapeDtypeStruct((height, LANES), jnp.bfloat16)

    same, following = pl.pallas_call(
        functools.partial(cells_kernel, cells=cells),
        out_shape=(table(cells + STAT_ROWS),) * 2,
        compiler_params=params(),
    )(flat)
    edge_same, edge_following = pl.pallas_call(
        functools.partial(edges_kernel, edges=edges, cols=cols),
        out_shape=(table(edges + STAT_ROWS),) * 2,
        scratch_shapes=[pltpu.VMEM((cells, LANES), jnp.float32)],
        compiler_params=params(),
    )(flat, gn_gain.reshape(1, chans), gn_bias.reshape(1, chans))

    route_a, route_b, edge_a, edge_b = [], [], [], []
    for s in range(n_blocks):
        h = s // 2
        hops = [
            (route_a, edge_a, h, near_of(s), h),
            (route_a, edge_a, 1 - h, far_of(s), h),
            (route_b, edge_b, h, s, 1 - h),
            (route_b, edge_b, 1 - h, mid_of(s), 1 - h),
        ]
        for route, edge_route, core, there, core_there in hops:
            route.append((2 * s + core, 2 * there + core_there))
            for x in range(2):
                edge_route.append((4 * s + 2 * x + core, 4 * there + 2 * (1 - x) + core_there))
    swap = [(0, 1), (1, 0)]
    got_b = lax.ppermute(same, ("tm", "chan"), route_b)
    got_a = lax.ppermute(following, ("tm", "chan"), route_a)
    got_edge_b = lax.ppermute(edge_same, ("tm", "tile", "chan"), edge_b)
    got_edge_a = lax.ppermute(edge_following, ("tm", "tile", "chan"), edge_a)

    def joined(first, second):
        return pl.pallas_call(
            join_kernel,
            out_shape=table(first.shape[0] + second.shape[0]),
            compiler_params=params(),
        )(first, second)

    got_d = lax.ppermute(joined(got_b, got_edge_b), "chan", swap)
    got_c = lax.ppermute(joined(got_a, got_edge_a), "chan", swap)
    spread = pl.pallas_call(
        functools.partial(spread_kernel, frames=frames, rows=rows, cols=cols, entries=entries),
        out_shape=jax.ShapeDtypeStruct((3, n_blocks * frames + 2, rows + 2, cols, LANES), jnp.bfloat16),
        scratch_shapes=[pltpu.VMEM(same.shape, jnp.bfloat16)],
        compiler_params=params(),
    )(same, got_a, got_edge_a, got_b, got_edge_b, got_c, got_d)

    weight = conv_weight.reshape(27 * LANES, outs)
    bias = conv_bias.reshape(1, outs)

    every = tuple(range(frames))

    def partial_sums(jobs, spans, adds=(), with_bias=False, dtype=jnp.bfloat16, after=None, cost=1):
        source = spread if after is None else lax.optimization_barrier((spread, after))[0]
        return pl.pallas_call(
            functools.partial(
                partial_kernel,
                jobs=jobs,
                n_adds=len(adds),
                n_outs=len(spans),
                frames=frames,
                rows=rows,
                cols=cols,
                with_bias=with_bias,
            ),
            out_shape=[jax.ShapeDtypeStruct((n * rows * cols, outs), dtype) for n in spans],
            compiler_params=params(),
            cost_estimate=pl.CostEstimate(flops=cost, transcendentals=0, bytes_accessed=1),
        )(source, weight, *adds, *([bias] if with_bias else []))

    def beyond_of(s):
        return far_of(near_of(s))

    near_route = [(s, near_of(s)) for s in range(n_blocks)]
    far_route = [(s, far_of(s)) for s in range(n_blocks)]
    parts = []
    for f in every:
        jobs, spans = [(beyond_of, f, 0, 0, None)], [1]
        if f == frames - 1:
            jobs += [(near_of, g, 1, g, None) for g in every]
            spans += [frames]
        parts.append(partial_sums(jobs, spans, after=parts[-1] if parts else None, cost=1 << 32))
    beyond = [lax.ppermute(part[0], "tm", near_route) for part in parts]
    sums = [partial_sums([(far_of, f, 0, 0, 0)], [1], (beyond[f],))[0] for f in every]
    arrived = [lax.ppermute(part, "tm", far_route) for part in sums]
    beside = lax.ppermute(parts[-1][1], "tm", near_route)
    home = partial_sums(
        [(lambda s: s, f, 0, f, None if f else 0) for f in every],
        [frames],
        arrived[:1],
        True,
        jnp.float32,
        cost=1 << 35,
    )[0]
    result = pl.pallas_call(
        functools.partial(finish_kernel, span=rows * cols),
        out_shape=jax.ShapeDtypeStruct((cells, outs), jnp.bfloat16),
        compiler_params=params(),
    )(home, beside, *arrived[1:])
    return result.reshape(frames, rows, cols, outs)


def splits(mesh):
    size = mesh.shape
    return size["tm"] == 4 and size["tile"] == 2 and size["chan"] == 2 and CH == size["tm"] * LANES


def solution(mesh):
    in_specs = (
        P(("groups", "tm"), None, "tile", "chan"),
        P("chan"),
        P("chan"),
        P(None, "tm", "chan"),
        P("chan"),
    )
    out_specs = P(("groups", "tm"), None, "tile", "chan")
    chosen = split_body if splits(mesh) else body
    return jax.shard_map(chosen, mesh=mesh, in_specs=in_specs, out_specs=out_specs, check_vma=False)
```

```python
import functools

import jax
import jax.numpy as jnp
from jax import lax
from jax.experimental import pallas as pl
from jax.experimental.pallas import tpu as pltpu
from jax.sharding import PartitionSpec as P

CH = 512
GROUPS = 32
EPS = 1e-06
LANES = 128
VMEM = 24 << 20
STAT_ROWS = 16


def shifted(block, axis, distance):
    devices = range(lax.axis_size(axis))
    route = [(i - distance, i) for i in devices if i - distance in devices]
    return lax.ppermute(block, axis, route)


def extended_2(cells, sides, width):
    for axis, dim in sides:
        count = lax.axis_size(axis)
        ends = count - 1
        head = lax.slice_in_dim(cells, 0, width, axis=dim)
        tail = lax.slice_in_dim(cells, cells.shape[dim] - width, cells.shape[dim], axis=dim)
        cells = jnp.concatenate(
            [
                lax.ppermute(tail, axis, [(i, (i + 1) % count) for i in range(ends)]),
                cells,
                lax.ppermute(head, axis, [((i + 1) % count, i) for i in range(ends)]),
            ],
            axis=dim,
        )
    return cells


def normalize(latent, gn_gain, gn_bias):
    values = latent.astype(jnp.float32)
    n_frames, n_rows, n_cols, n_chans = latent.shape
    group_ch = CH // GROUPS
    local_groups = n_chans // group_ch
    shaped = values.reshape(n_frames, n_rows, n_cols, local_groups, group_ch)
    part_sum = jnp.sum(shaped, axis=(0, 1, 2, 4))
    part_square = jnp.sum(shaped * shaped, axis=(0, 1, 2, 4))
    total_sum, total_square = lax.psum((part_sum, part_square), ("tm", "tile"))
    entries = n_frames * n_rows * n_cols * group_ch * lax.axis_size("tm") * lax.axis_size("tile")
    mean_grp = total_sum / entries
    square_grp = total_square / entries
    inv_grp = lax.rsqrt(square_grp - mean_grp * mean_grp + 1e-06)
    mean_ch = jnp.repeat(mean_grp, group_ch)
    inv_ch = jnp.repeat(inv_grp, group_ch)
    scaled = (values - mean_ch) * inv_ch * gn_gain.astype(jnp.float32) + gn_bias.astype(jnp.float32)
    return jax.nn.silu(scaled).astype(jnp.bfloat16)


def conv_term(padded, n_frames, n_rows, n_cols, block_in):
    width_in = block_in.shape[1]
    columns = [
        padded[
            time_off : time_off + n_frames, row_off : row_off + n_rows, col_off : col_off + n_cols
        ]
        for time_off in range(3)
        for row_off in range(3)
        for col_off in range(3)
    ]
    stacked = jnp.stack(columns, axis=3).reshape(n_frames * n_rows * n_cols, 27 * width_in)
    matrix = block_in.reshape(27 * width_in, block_in.shape[2])
    return jnp.dot(stacked, matrix, preferred_element_type=jnp.float32)


def body(latent, gn_gain, gn_bias, conv_weight, conv_bias):
    n_frames, n_rows, n_cols, n_chans = latent.shape
    normed = normalize(latent, gn_gain, gn_bias)
    full_feat = lax.all_gather(normed, "chan", axis=3, tiled=True)
    earlier = shifted(full_feat, "tm", 1)
    extended = jnp.concatenate([earlier, full_feat], axis=0)
    rimmed = extended_2(extended, (("tile", 2),), 1)
    padded = jnp.pad(rimmed, ((0, 0), (1, 1), (0, 0), (0, 0)))
    summed = conv_term(
        padded, n_frames, n_rows, n_cols, lax.all_gather(conv_weight, "tm", axis=1, tiled=True)
    )
    result = (summed + conv_bias.astype(jnp.float32)).astype(jnp.bfloat16)
    return result.reshape(n_frames, n_rows, n_cols, n_chans)


def near_of(s):
    return s + 1 - 2 * (s % 2)


def mid_of(s):
    return (s + 2) % 4


def far_of(s):
    return 3 - s


def three(value):
    high = value.astype(jnp.bfloat16)
    rest = value - high.astype(jnp.float32)
    mid = rest.astype(jnp.bfloat16)
    low = (rest - mid.astype(jnp.float32)).astype(jnp.bfloat16)
    return [high.astype(jnp.float32), mid.astype(jnp.float32), low.astype(jnp.float32)]


def tail_rows(rows):
    rows = jnp.concatenate(rows, axis=0)
    filler = jnp.zeros((STAT_ROWS - rows.shape[0], rows.shape[1]), jnp.float32)
    return jnp.concatenate([rows, filler], axis=0).astype(jnp.bfloat16)


def sum_rows(wide):
    total = jnp.sum(wide, axis=0, keepdims=True)
    square = jnp.sum(wide * wide, axis=0, keepdims=True)
    return three(total) + three(square)


def by_parity(fill):
    parity = lax.axis_index("tm") % 2

    @pl.when(parity == 0)
    def _():
        fill(slice(0, LANES), slice(LANES, 2 * LANES))

    @pl.when(parity == 1)
    def _():
        fill(slice(LANES, 2 * LANES), slice(0, LANES))


def cells_kernel(latent_ref, same_ref, next_ref, *, cells):
    def fill(same, following):
        for out_ref, lanes in ((same_ref, same), (next_ref, following)):
            out_ref[:cells] = latent_ref[:, lanes]
            out_ref[cells:] = tail_rows(sum_rows(latent_ref[:, lanes].astype(jnp.float32)))

    by_parity(fill)


def edges_kernel(latent_ref, gain_ref, bias_ref, same_ref, next_ref, wide_ref, *, edges, cols):
    first = jnp.where(lax.axis_index("tile") == 0, cols - 1, 0)

    def fill(same, following):
        for out_ref, lanes in ((same_ref, same), (next_ref, following)):
            wide = latent_ref[:, lanes].astype(jnp.float32)
            wide_ref[...] = wide
            out_ref[:edges] = wide_ref[pl.ds(first, edges, stride=cols), :].astype(jnp.bfloat16)
            params_rows = [ref[:, lanes].astype(jnp.float32) for ref in (gain_ref, bias_ref)]
            out_ref[edges:] = tail_rows(sum_rows(wide) + params_rows)

    by_parity(fill)


def join_kernel(*refs):
    out_ref = refs[-1]
    at = 0
    for ref in refs[:-1]:
        out_ref[at : at + ref.shape[0]] = ref[...]
        at += ref.shape[0]


def group_total(row, group_ch):
    lane = lax.broadcasted_iota(jnp.int32, row.shape, 1)
    step = 1
    while step < group_ch:
        up = pltpu.roll(row, LANES - step, 1)
        down = pltpu.roll(row, step, 1)
        row = row + jnp.where((lane // step) % 2 == 0, up, down)
        step *= 2
    return row


def spread_kernel(
    same_ref, a_ref, edge_a_ref, b_ref, edge_b_ref, swapped_ref, out_ref, own_ref,
    *, frames, rows, cols, entries, first,
):
    s = lax.axis_index("tm")
    home = lax.axis_index("chan") == s // 2
    tile = lax.axis_index("tile")
    cells = frames * rows * cols
    edges = frames * rows
    split = cells + STAT_ROWS
    height = split + edges + STAT_ROWS

    @pl.when(home)
    def _():
        own_ref[...] = same_ref[...]

    @pl.when(jnp.logical_not(home))
    def _():
        own_ref[...] = swapped_ref[height : height + split]

    near, mid, far = near_of(s), mid_of(s), far_of(s)
    pieces = (
        (own_ref, swapped_ref, height + split, jnp.where(home, s, mid)),
        (a_ref, edge_a_ref, 0, jnp.where(home, near, far)),
        (b_ref, edge_b_ref, 0, jnp.where(home, mid, s)),
        (swapped_ref, swapped_ref, split, jnp.where(home, far, near)),
    )
    stats = jnp.zeros((STAT_ROWS, LANES), jnp.float32)
    for ref, edge_ref, skip, _ in pieces:
        last = edge_ref[skip + edges : skip + edges + STAT_ROWS].astype(jnp.float32)
        stats = stats + ref[cells : cells + STAT_ROWS].astype(jnp.float32) + last
    total = group_total(stats[0:1] + stats[1:2] + stats[2:3], CH // GROUPS) / entries
    square = group_total(stats[3:4] + stats[4:5] + stats[5:6], CH // GROUPS) / entries
    scale = lax.rsqrt(square - total * total + EPS) * last[6:7]
    shift = last[7:8]

    def normed(raw):
        value = (raw.astype(jnp.float32) - total) * scale + shift
        return value / (1.0 + jnp.exp(-value))

    n_all = out_ref.shape[1]
    zero_row = jnp.zeros((cols, LANES), jnp.bfloat16)
    for d in range(3):
        for f in range(n_all):
            out_ref[d, f, 0] = zero_row
            out_ref[d, f, rows + 1] = zero_row

    def clear():
        for d in range(3):
            for f in range(2):
                out_ref[d, f, 1 : rows + 1] = jnp.zeros((rows, cols, LANES), jnp.bfloat16)

    col = lax.broadcasted_iota(jnp.int32, (rows, cols, LANES), 1)
    span = rows * cols

    def place(ref, edge_ref, skip, start):
        for f in range(frames):
            value = normed(ref[f * span : (f + 1) * span])
            edge = normed(edge_ref[skip + f * rows : skip + (f + 1) * rows])
            edge = jnp.broadcast_to(edge[:, None, :], (rows, cols, LANES))
            left = pltpu.roll(value, 1, 0).reshape(rows, cols, LANES)
            left = jnp.where(col == 0, jnp.where(tile == 1, edge, 0.0), left)
            right = pltpu.roll(value, span - 1, 0).reshape(rows, cols, LANES)
            right = jnp.where(col == cols - 1, jnp.where(tile == 0, edge, 0.0), right)
            at = start + f
            out_ref[0, at, 1 : rows + 1] = left.astype(jnp.bfloat16)
            out_ref[1, at, 1 : rows + 1] = value.reshape(rows, cols, LANES).astype(jnp.bfloat16)
            out_ref[2, at, 1 : rows + 1] = right.astype(jnp.bfloat16)

    if first:
        pl.when(mid == 0)(clear)
        for ref, edge_ref, skip, block in pieces:
            wanted = jnp.logical_or(block == mid, block == mid - 1)
            start = (block - mid + 1) * frames
            pl.when(wanted)(functools.partial(place, ref, edge_ref, skip, start))
    else:
        clear()
        for ref, edge_ref, skip, block in pieces:
            place(ref, edge_ref, skip, 2 + block * frames)


def partial_kernel(spread_ref, weight_ref, *rest, jobs, n_adds, n_outs, frames, rows, cols, with_bias):
    outs = rest[len(rest) - n_outs :]
    s = lax.axis_index("tm")
    span = rows * cols
    for block_of, f, out, place, added in jobs:
        at = block_of(s) * frames + f
        stacked = jnp.concatenate(
            [
                spread_ref[d, at + a, b : b + rows].reshape(span, LANES)
                for a in range(3)
                for b in range(3)
                for d in range(3)
            ],
            axis=1,
        )
        total = jnp.dot(stacked, weight_ref[...], preferred_element_type=jnp.float32)
        for ref, core in added:
            more = rest[ref][...].astype(jnp.float32)
            total = total + (more if core is None else jnp.where(lax.axis_index("chan") == core, more, 0.0))
        if with_bias:
            total = total + rest[n_adds][...].astype(jnp.float32)
        outs[out][place * span : (place + 1) * span] = total.astype(outs[out].dtype)


def finish_kernel(*refs):
    last_ref, out_ref = refs[-2:]
    span = last_ref.shape[0]
    for k, ref in enumerate(refs[:-2]):
        total = ref[...]
        if k == len(refs) - 3:
            total = total + last_ref[...].astype(jnp.float32)
        out_ref[k * span : (k + 1) * span] = total.astype(out_ref.dtype)


def params():
    return pltpu.CompilerParams(vmem_limit_bytes=VMEM)


def split_body(latent, gn_gain, gn_bias, conv_weight, conv_bias):
    frames, rows, cols, chans = latent.shape
    outs = conv_weight.shape[2]
    cells = frames * rows * cols
    edges = frames * rows
    n_blocks = lax.axis_size("tm")
    entries = cells * n_blocks * lax.axis_size("tile") * (CH // GROUPS)
    flat = latent.reshape(cells, chans)

    def table(height):
        return jax.ShapeDtypeStruct((height, LANES), jnp.bfloat16)

    same, following = pl.pallas_call(
        functools.partial(cells_kernel, cells=cells),
        out_shape=(table(cells + STAT_ROWS),) * 2,
        compiler_params=params(),
    )(flat)
    edge_same, edge_following = pl.pallas_call(
        functools.partial(edges_kernel, edges=edges, cols=cols),
        out_shape=(table(edges + STAT_ROWS),) * 2,
        scratch_shapes=[pltpu.VMEM((cells, LANES), jnp.float32)],
        compiler_params=params(),
    )(flat, gn_gain.reshape(1, chans), gn_bias.reshape(1, chans))

    route_a, route_b, edge_a, edge_b = [], [], [], []
    for s in range(n_blocks):
        h = s // 2
        hops = [
            (route_a, edge_a, h, near_of(s), h),
            (route_a, edge_a, 1 - h, far_of(s), h),
            (route_b, edge_b, h, s, 1 - h),
            (route_b, edge_b, 1 - h, mid_of(s), 1 - h),
        ]
        for route, edge_route, core, there, core_there in hops:
            route.append((2 * s + core, 2 * there + core_there))
            for x in range(2):
                edge_route.append((4 * s + 2 * x + core, 4 * there + 2 * (1 - x) + core_there))
    swap = [(0, 1), (1, 0)]
    both = ("tm", "chan")
    got_b = lax.ppermute(same, both, route_b)
    got_a = lax.ppermute(following, both, route_a)
    got_edge_b = lax.ppermute(edge_same, ("tm", "tile", "chan"), edge_b)
    got_edge_a = lax.ppermute(edge_following, ("tm", "tile", "chan"), edge_a)

    received = (got_a, got_edge_a, got_b, got_edge_b)
    joined = pl.pallas_call(
        join_kernel,
        out_shape=table(sum(part.shape[0] for part in received)),
        compiler_params=params(),
    )(*received)
    swapped = lax.ppermute(joined, "chan", swap)

    def spread_out(n_frames, first, after=None):
        head = same if after is None else lax.optimization_barrier((same, after))[0]
        return pl.pallas_call(
            functools.partial(
                spread_kernel, frames=frames, rows=rows, cols=cols, entries=entries, first=first
            ),
            out_shape=jax.ShapeDtypeStruct((3, n_frames, rows + 2, cols, LANES), jnp.bfloat16),
            scratch_shapes=[pltpu.VMEM(same.shape, jnp.bfloat16)],
            compiler_params=params(),
        )(head, *received, swapped)

    narrow = spread_out(2 + frames, True)

    weight = conv_weight.reshape(27 * LANES, outs)
    bias = conv_bias.reshape(1, outs)

    every = tuple(range(frames))

    def partial_sums(acts, jobs, spans, adds=(), with_bias=False, dtype=jnp.bfloat16, after=None, cost=1):
        source = acts if after is None else lax.optimization_barrier((acts, after))[0]
        return pl.pallas_call(
            functools.partial(
                partial_kernel,
                jobs=jobs,
                n_adds=len(adds),
                n_outs=len(spans),
                frames=frames,
                rows=rows,
                cols=cols,
                with_bias=with_bias,
            ),
            out_shape=[jax.ShapeDtypeStruct((n * rows * cols, outs), dtype) for n in spans],
            compiler_params=params(),
            cost_estimate=pl.CostEstimate(flops=cost, transcendentals=0, bytes_accessed=1),
        )(source, weight, *adds, *([bias] if with_bias else []))

    def beyond_of(s):
        return far_of(near_of(s))

    def mixed(core):
        return lambda s: jnp.where(lax.axis_index("chan") == core, far_of(s), near_of(s))

    near_route = [(s, near_of(s)) for s in range(n_blocks)]
    mixed_route = [
        [
            (2 * s + c, 2 * (far_of(s) if c == core else near_of(s)) + c)
            for s in range(n_blocks)
            for c in range(2)
        ]
        for core in range(2)
    ]
    parts = partial_sums(narrow, [(lambda s: 0, 0, 0, 0, ())], [1], cost=1 << 32)
    spread = spread_out(2 + n_blocks * frames, False, parts[0])
    for f in every[1:]:
        parts += partial_sums(spread, [(beyond_of, f, 0, 0, ())], [1], after=parts, cost=1 << 32)
    beyond = [lax.ppermute(part, "tm", near_route) for part in parts]
    arrived, sums = [], None
    for f in every:
        jobs = [(mixed(core), f, core, 0, ((0, core),)) for core in range(2)]
        sums = partial_sums(spread, jobs, [1, 1], (beyond[f],), after=sums)
        arrived += [lax.ppermute(part, both, route) for part, route in zip(sums, mixed_route)]
    home = []
    for f in every:
        adds = arrived[2 * f : 2 * f + 2] if f < frames - 1 else arrived[2 * f : 2 * f + 1]
        jobs = [(lambda s: s, f, 0, 0, tuple((k, None) for k in range(len(adds))))]
        after = home or None
        home += partial_sums(spread, jobs, [1], adds, True, jnp.float32, after=after, cost=1 << 35)
    result = pl.pallas_call(
        finish_kernel,
        out_shape=jax.ShapeDtypeStruct((cells, outs), jnp.bfloat16),
        compiler_params=params(),
    )(*home, arrived[-1])
    return result.reshape(frames, rows, cols, outs)


def splits(mesh):
    size = mesh.shape
    return size["tm"] == 4 and size["tile"] == 2 and size["chan"] == 2 and CH == size["tm"] * LANES


def solution(mesh):
    in_specs = (
        P(("groups", "tm"), None, "tile", "chan"),
        P("chan"),
        P("chan"),
        P(None, "tm", "chan"),
        P("chan"),
    )
    out_specs = P(("groups", "tm"), None, "tile", "chan")
    chosen = split_body if splits(mesh) else body
    return jax.shard_map(chosen, mesh=mesh, in_specs=in_specs, out_specs=out_specs, check_vma=False)
```

```python
import functools

import jax
import jax.numpy as jnp
from jax import lax
from jax.experimental import pallas as pl
from jax.experimental.pallas import tpu as pltpu
from jax.sharding import PartitionSpec as P

CH = 512
GROUPS = 32
EPS = 1e-06
LANES = 128
VMEM = 24 << 20
STAT_ROWS = 16


def shifted(block, axis, distance):
    devices = range(lax.axis_size(axis))
    route = [(i - distance, i) for i in devices if i - distance in devices]
    return lax.ppermute(block, axis, route)


def extended_2(cells, sides, width):
    for axis, dim in sides:
        count = lax.axis_size(axis)
        ends = count - 1
        head = lax.slice_in_dim(cells, 0, width, axis=dim)
        tail = lax.slice_in_dim(cells, cells.shape[dim] - width, cells.shape[dim], axis=dim)
        cells = jnp.concatenate(
            [
                lax.ppermute(tail, axis, [(i, (i + 1) % count) for i in range(ends)]),
                cells,
                lax.ppermute(head, axis, [((i + 1) % count, i) for i in range(ends)]),
            ],
            axis=dim,
        )
    return cells


def normalize(latent, gn_gain, gn_bias):
    values = latent.astype(jnp.float32)
    n_frames, n_rows, n_cols, n_chans = latent.shape
    group_ch = CH // GROUPS
    local_groups = n_chans // group_ch
    shaped = values.reshape(n_frames, n_rows, n_cols, local_groups, group_ch)
    part_sum = jnp.sum(shaped, axis=(0, 1, 2, 4))
    part_square = jnp.sum(shaped * shaped, axis=(0, 1, 2, 4))
    total_sum, total_square = lax.psum((part_sum, part_square), ("tm", "tile"))
    entries = n_frames * n_rows * n_cols * group_ch * lax.axis_size("tm") * lax.axis_size("tile")
    mean_grp = total_sum / entries
    square_grp = total_square / entries
    inv_grp = lax.rsqrt(square_grp - mean_grp * mean_grp + 1e-06)
    mean_ch = jnp.repeat(mean_grp, group_ch)
    inv_ch = jnp.repeat(inv_grp, group_ch)
    scaled = (values - mean_ch) * inv_ch * gn_gain.astype(jnp.float32) + gn_bias.astype(jnp.float32)
    return jax.nn.silu(scaled).astype(jnp.bfloat16)


def conv_term(padded, n_frames, n_rows, n_cols, block_in):
    width_in = block_in.shape[1]
    columns = [
        padded[
            time_off : time_off + n_frames, row_off : row_off + n_rows, col_off : col_off + n_cols
        ]
        for time_off in range(3)
        for row_off in range(3)
        for col_off in range(3)
    ]
    stacked = jnp.stack(columns, axis=3).reshape(n_frames * n_rows * n_cols, 27 * width_in)
    matrix = block_in.reshape(27 * width_in, block_in.shape[2])
    return jnp.dot(stacked, matrix, preferred_element_type=jnp.float32)


def body(latent, gn_gain, gn_bias, conv_weight, conv_bias):
    n_frames, n_rows, n_cols, n_chans = latent.shape
    normed = normalize(latent, gn_gain, gn_bias)
    full_feat = lax.all_gather(normed, "chan", axis=3, tiled=True)
    earlier = shifted(full_feat, "tm", 1)
    extended = jnp.concatenate([earlier, full_feat], axis=0)
    rimmed = extended_2(extended, (("tile", 2),), 1)
    padded = jnp.pad(rimmed, ((0, 0), (1, 1), (0, 0), (0, 0)))
    summed = conv_term(
        padded, n_frames, n_rows, n_cols, lax.all_gather(conv_weight, "tm", axis=1, tiled=True)
    )
    result = (summed + conv_bias.astype(jnp.float32)).astype(jnp.bfloat16)
    return result.reshape(n_frames, n_rows, n_cols, n_chans)


def near_of(s):
    return s + 1 - 2 * (s % 2)


def mid_of(s):
    return (s + 2) % 4


def far_of(s):
    return 3 - s


def three(value):
    high = value.astype(jnp.bfloat16)
    rest = value - high.astype(jnp.float32)
    mid = rest.astype(jnp.bfloat16)
    low = (rest - mid.astype(jnp.float32)).astype(jnp.bfloat16)
    return [high.astype(jnp.float32), mid.astype(jnp.float32), low.astype(jnp.float32)]


def tail_rows(rows):
    rows = jnp.concatenate(rows, axis=0)
    filler = jnp.zeros((STAT_ROWS - rows.shape[0], rows.shape[1]), jnp.float32)
    return jnp.concatenate([rows, filler], axis=0).astype(jnp.bfloat16)


def sum_rows(wide):
    total = jnp.sum(wide, axis=0, keepdims=True)
    square = jnp.sum(wide * wide, axis=0, keepdims=True)
    return three(total) + three(square)


def by_parity(fill):
    parity = lax.axis_index("tm") % 2

    @pl.when(parity == 0)
    def _():
        fill(slice(0, LANES), slice(LANES, 2 * LANES))

    @pl.when(parity == 1)
    def _():
        fill(slice(LANES, 2 * LANES), slice(0, LANES))


def cells_kernel(latent_ref, same_ref, next_ref, *, cells):
    def fill(same, following):
        for out_ref, lanes in ((same_ref, same), (next_ref, following)):
            out_ref[:cells] = latent_ref[:, lanes]
            out_ref[cells:] = tail_rows(sum_rows(latent_ref[:, lanes].astype(jnp.float32)))

    by_parity(fill)


def edges_kernel(latent_ref, gain_ref, bias_ref, same_ref, next_ref, wide_ref, *, edges, cols):
    first = jnp.where(lax.axis_index("tile") == 0, cols - 1, 0)

    def fill(same, following):
        for out_ref, lanes in ((same_ref, same), (next_ref, following)):
            wide = latent_ref[:, lanes].astype(jnp.float32)
            wide_ref[...] = wide
            out_ref[:edges] = wide_ref[pl.ds(first, edges, stride=cols), :].astype(jnp.bfloat16)
            params_rows = [ref[:, lanes].astype(jnp.float32) for ref in (gain_ref, bias_ref)]
            out_ref[edges:] = tail_rows(sum_rows(wide) + params_rows)

    by_parity(fill)


def join_kernel(*refs):
    out_ref = refs[-1]
    at = 0
    for ref in refs[:-1]:
        out_ref[at : at + ref.shape[0]] = ref[...]
        at += ref.shape[0]


def group_total(row, group_ch):
    lane = lax.broadcasted_iota(jnp.int32, row.shape, 1)
    step = 1
    while step < group_ch:
        up = pltpu.roll(row, LANES - step, 1)
        down = pltpu.roll(row, step, 1)
        row = row + jnp.where((lane // step) % 2 == 0, up, down)
        step *= 2
    return row


def spread_kernel(
    same_ref, a_ref, edge_a_ref, b_ref, edge_b_ref, swapped_ref, out_ref, own_ref,
    *, frames, rows, cols, entries, first,
):
    s = lax.axis_index("tm")
    home = lax.axis_index("chan") == s // 2
    tile = lax.axis_index("tile")
    cells = frames * rows * cols
    edges = frames * rows
    split = cells + STAT_ROWS
    height = split + edges + STAT_ROWS

    @pl.when(home)
    def _():
        own_ref[...] = same_ref[...]

    @pl.when(jnp.logical_not(home))
    def _():
        own_ref[...] = swapped_ref[height : height + split]

    near, mid, far = near_of(s), mid_of(s), far_of(s)
    pieces = (
        (own_ref, swapped_ref, height + split, jnp.where(home, s, mid)),
        (a_ref, edge_a_ref, 0, jnp.where(home, near, far)),
        (b_ref, edge_b_ref, 0, jnp.where(home, mid, s)),
        (swapped_ref, swapped_ref, split, jnp.where(home, far, near)),
    )
    stats = jnp.zeros((STAT_ROWS, LANES), jnp.float32)
    for ref, edge_ref, skip, _ in pieces:
        last = edge_ref[skip + edges : skip + edges + STAT_ROWS].astype(jnp.float32)
        stats = stats + ref[cells : cells + STAT_ROWS].astype(jnp.float32) + last
    total = group_total(stats[0:1] + stats[1:2] + stats[2:3], CH // GROUPS) / entries
    square = group_total(stats[3:4] + stats[4:5] + stats[5:6], CH // GROUPS) / entries
    scale = lax.rsqrt(square - total * total + EPS) * last[6:7]
    shift = last[7:8]

    def normed(raw):
        value = (raw.astype(jnp.float32) - total) * scale + shift
        return value / (1.0 + jnp.exp(-value))

    n_all = out_ref.shape[1]
    zero_row = jnp.zeros((cols, LANES), jnp.bfloat16)
    for d in range(3):
        for f in range(n_all):
            out_ref[d, f, 0] = zero_row
            out_ref[d, f, rows + 1] = zero_row

    def clear():
        for d in range(3):
            for f in range(2):
                out_ref[d, f, 1 : rows + 1] = jnp.zeros((rows, cols, LANES), jnp.bfloat16)

    col = lax.broadcasted_iota(jnp.int32, (rows, cols, LANES), 1)
    span = rows * cols

    def place(ref, edge_ref, skip, start):
        for f in range(frames):
            value = normed(ref[f * span : (f + 1) * span])
            edge = normed(edge_ref[skip + f * rows : skip + (f + 1) * rows])
            edge = jnp.broadcast_to(edge[:, None, :], (rows, cols, LANES))
            left = pltpu.roll(value, 1, 0).reshape(rows, cols, LANES)
            left = jnp.where(col == 0, jnp.where(tile == 1, edge, 0.0), left)
            right = pltpu.roll(value, span - 1, 0).reshape(rows, cols, LANES)
            right = jnp.where(col == cols - 1, jnp.where(tile == 0, edge, 0.0), right)
            at = start + f
            out_ref[0, at, 1 : rows + 1] = left.astype(jnp.bfloat16)
            out_ref[1, at, 1 : rows + 1] = value.reshape(rows, cols, LANES).astype(jnp.bfloat16)
            out_ref[2, at, 1 : rows + 1] = right.astype(jnp.bfloat16)

    if first:
        target = jnp.where(lax.axis_index("chan") == 0, far, mid)
        pl.when(target == 0)(clear)
        for ref, edge_ref, skip, block in pieces:
            wanted = jnp.logical_or(block == target, block == target - 1)
            start = (block - target + 1) * frames
            pl.when(wanted)(functools.partial(place, ref, edge_ref, skip, start))
    else:
        clear()
        for ref, edge_ref, skip, block in pieces:
            place(ref, edge_ref, skip, 2 + block * frames)


def partial_kernel(spread_ref, weight_ref, *rest, jobs, n_adds, n_outs, frames, rows, cols, with_bias):
    outs = rest[len(rest) - n_outs :]
    s = lax.axis_index("tm")
    span = rows * cols
    for frame_of, out, place, added in jobs:
        at = frame_of(s)
        stacked = jnp.concatenate(
            [
                spread_ref[d, at + a, b : b + rows].reshape(span, LANES)
                for a in range(3)
                for b in range(3)
                for d in range(3)
            ],
            axis=1,
        )
        total = jnp.dot(stacked, weight_ref[...], preferred_element_type=jnp.float32)
        for ref, core in added:
            more = rest[ref][...].astype(jnp.float32)
            total = total + (more if core is None else jnp.where(lax.axis_index("chan") == core, more, 0.0))
        if with_bias:
            total = total + rest[n_adds][...].astype(jnp.float32)
        outs[out][place * span : (place + 1) * span] = total.astype(outs[out].dtype)


def finish_kernel(first_ref, second_ref, one_ref, other_ref, out_ref):
    span = first_ref.shape[0]
    out_ref[:span] = first_ref[...].astype(out_ref.dtype)
    total = second_ref[...] + one_ref[...].astype(jnp.float32) + other_ref[...].astype(jnp.float32)
    out_ref[span:] = total.astype(out_ref.dtype)


def params():
    return pltpu.CompilerParams(vmem_limit_bytes=VMEM)


def split_body(latent, gn_gain, gn_bias, conv_weight, conv_bias):
    frames, rows, cols, chans = latent.shape
    if frames != 2:
        return body(latent, gn_gain, gn_bias, conv_weight, conv_bias)
    outs = conv_weight.shape[2]
    cells = frames * rows * cols
    edges = frames * rows
    n_blocks = lax.axis_size("tm")
    entries = cells * n_blocks * lax.axis_size("tile") * (CH // GROUPS)
    flat = latent.reshape(cells, chans)

    def table(height):
        return jax.ShapeDtypeStruct((height, LANES), jnp.bfloat16)

    same, following = pl.pallas_call(
        functools.partial(cells_kernel, cells=cells),
        out_shape=(table(cells + STAT_ROWS),) * 2,
        compiler_params=params(),
    )(flat)
    edge_same, edge_following = pl.pallas_call(
        functools.partial(edges_kernel, edges=edges, cols=cols),
        out_shape=(table(edges + STAT_ROWS),) * 2,
        scratch_shapes=[pltpu.VMEM((cells, LANES), jnp.float32)],
        compiler_params=params(),
    )(flat, gn_gain.reshape(1, chans), gn_bias.reshape(1, chans))

    route_a, route_b, edge_a, edge_b = [], [], [], []
    for s in range(n_blocks):
        h = s // 2
        hops = [
            (route_a, edge_a, h, near_of(s), h),
            (route_a, edge_a, 1 - h, far_of(s), h),
            (route_b, edge_b, h, s, 1 - h),
            (route_b, edge_b, 1 - h, mid_of(s), 1 - h),
        ]
        for route, edge_route, core, there, core_there in hops:
            route.append((2 * s + core, 2 * there + core_there))
            for x in range(2):
                edge_route.append((4 * s + 2 * x + core, 4 * there + 2 * (1 - x) + core_there))
    swap = [(0, 1), (1, 0)]
    both = ("tm", "chan")
    got_b = lax.ppermute(same, both, route_b)
    got_a = lax.ppermute(following, both, route_a)
    got_edge_b = lax.ppermute(edge_same, ("tm", "tile", "chan"), edge_b)
    got_edge_a = lax.ppermute(edge_following, ("tm", "tile", "chan"), edge_a)

    received = (got_a, got_edge_a, got_b, got_edge_b)
    joined = pl.pallas_call(
        join_kernel,
        out_shape=table(sum(part.shape[0] for part in received)),
        compiler_params=params(),
    )(*received)
    swapped = lax.ppermute(joined, "chan", swap)

    def spread_out(n_frames, first, after=None):
        head = same if after is None else lax.optimization_barrier((same, after))[0]
        return pl.pallas_call(
            functools.partial(
                spread_kernel, frames=frames, rows=rows, cols=cols, entries=entries, first=first
            ),
            out_shape=jax.ShapeDtypeStruct((3, n_frames, rows + 2, cols, LANES), jnp.bfloat16),
            scratch_shapes=[pltpu.VMEM(same.shape, jnp.bfloat16)],
            compiler_params=params(),
        )(head, *received, swapped)

    narrow = spread_out(2 + frames, True)

    weight = conv_weight.reshape(27 * LANES, outs)
    bias = conv_bias.reshape(1, outs)

    def partial_sums(acts, jobs, spans, adds=(), with_bias=False, dtype=jnp.bfloat16, after=None, cost=1):
        source = acts if after is None else lax.optimization_barrier((acts, after))[0]
        return pl.pallas_call(
            functools.partial(
                partial_kernel,
                jobs=jobs,
                n_adds=len(adds),
                n_outs=len(spans),
                frames=frames,
                rows=rows,
                cols=cols,
                with_bias=with_bias,
            ),
            out_shape=[jax.ShapeDtypeStruct((n * rows * cols, outs), dtype) for n in spans],
            compiler_params=params(),
            cost_estimate=pl.CostEstimate(flops=cost, transcendentals=0, bytes_accessed=1),
        )(source, weight, *adds, *([bias] if with_bias else []))

    def mixed(core, ours, theirs):
        return lambda s: jnp.where(lax.axis_index("chan") == core, ours(s), theirs(s))

    def frame(block_of, f):
        return lambda s: block_of(s) * frames + f

    def route(core, goal):
        return [
            (2 * s + c, 2 * (goal(s) if c == core else near_of(s)) + c)
            for s in range(n_blocks)
            for c in range(2)
        ]

    lead = partial_sums(narrow, [(mixed(0, lambda s: 0, lambda s: 1), 0, 0, ())], [1], cost=1 << 32)
    spread = spread_out(2 + n_blocks * frames, False, lead[0])
    second = mixed(1, frame(far_of, 0), frame(mid_of, 1))
    second = partial_sums(spread, [(second, 0, 0, ())], [1], after=lead, cost=1 << 32)
    jobs = [(mixed(core, frame(mid_of, 0), frame(near_of, 0)), core, 0, ()) for core in range(2)]
    straight = partial_sums(spread, jobs, [1, 1], after=second, cost=1 << 32)
    got_1 = lax.ppermute(lead[0], both, route(0, far_of))
    got_2 = lax.ppermute(second[0], both, route(1, far_of))
    got_3 = lax.ppermute(straight[0], both, route(0, mid_of))
    got_4 = lax.ppermute(straight[1], both, route(1, mid_of))
    last = [
        partial_sums(
            spread, [(mixed(core, frame(far_of, 1), frame(near_of, 1)), 0, 0, ((0, core),))], [1], (got,), after=after
        )[0]
        for core, got, after in ((0, got_2, straight), (1, got_1, got_2))
    ]
    got_5, got_6 = [lax.ppermute(sent, both, route(core, far_of)) for core, sent in enumerate(last)]
    home = []
    for f, adds, added in (
        (0, (got_1, got_2, got_3, got_4), ((0, 0), (1, 1), (2, None), (3, None))),
        (1, (), ()),
    ):
        jobs = [(frame(lambda s: s, f), 0, 0, added)]
        after = home or None
        home += partial_sums(spread, jobs, [1], adds, True, jnp.float32, after=after, cost=1 << 35)
    result = pl.pallas_call(
        finish_kernel,
        out_shape=jax.ShapeDtypeStruct((cells, outs), jnp.bfloat16),
        compiler_params=params(),
    )(*home, got_5, got_6)
    return result.reshape(frames, rows, cols, outs)


def splits(mesh):
    size = mesh.shape
    return size["tm"] == 4 and size["tile"] == 2 and size["chan"] == 2 and CH == size["tm"] * LANES


def solution(mesh):
    in_specs = (
        P(("groups", "tm"), None, "tile", "chan"),
        P("chan"),
        P("chan"),
        P(None, "tm", "chan"),
        P("chan"),
    )
    out_specs = P(("groups", "tm"), None, "tile", "chan")
    chosen = split_body if splits(mesh) else body
    return jax.shard_map(chosen, mesh=mesh, in_specs=in_specs, out_specs=out_specs, check_vma=False)
```

```python
import functools

import jax
import jax.numpy as jnp
from jax import lax
from jax.experimental import pallas as pl
from jax.experimental.pallas import tpu as pltpu
from jax.sharding import PartitionSpec as P

CH = 512
GROUPS = 32
EPS = 1e-06
LANES = 128
VMEM = 24 << 20
STAT_ROWS = 16


def shifted(block, axis, distance):
    devices = range(lax.axis_size(axis))
    route = [(i - distance, i) for i in devices if i - distance in devices]
    return lax.ppermute(block, axis, route)


def extended_2(cells, sides, width):
    for axis, dim in sides:
        count = lax.axis_size(axis)
        ends = count - 1
        head = lax.slice_in_dim(cells, 0, width, axis=dim)
        tail = lax.slice_in_dim(cells, cells.shape[dim] - width, cells.shape[dim], axis=dim)
        cells = jnp.concatenate(
            [
                lax.ppermute(tail, axis, [(i, (i + 1) % count) for i in range(ends)]),
                cells,
                lax.ppermute(head, axis, [((i + 1) % count, i) for i in range(ends)]),
            ],
            axis=dim,
        )
    return cells


def normalize(latent, gn_gain, gn_bias):
    values = latent.astype(jnp.float32)
    n_frames, n_rows, n_cols, n_chans = latent.shape
    group_ch = CH // GROUPS
    local_groups = n_chans // group_ch
    shaped = values.reshape(n_frames, n_rows, n_cols, local_groups, group_ch)
    part_sum = jnp.sum(shaped, axis=(0, 1, 2, 4))
    part_square = jnp.sum(shaped * shaped, axis=(0, 1, 2, 4))
    total_sum, total_square = lax.psum((part_sum, part_square), ("tm", "tile"))
    entries = n_frames * n_rows * n_cols * group_ch * lax.axis_size("tm") * lax.axis_size("tile")
    mean_grp = total_sum / entries
    square_grp = total_square / entries
    inv_grp = lax.rsqrt(square_grp - mean_grp * mean_grp + 1e-06)
    mean_ch = jnp.repeat(mean_grp, group_ch)
    inv_ch = jnp.repeat(inv_grp, group_ch)
    scaled = (values - mean_ch) * inv_ch * gn_gain.astype(jnp.float32) + gn_bias.astype(jnp.float32)
    return jax.nn.silu(scaled).astype(jnp.bfloat16)


def conv_term(padded, n_frames, n_rows, n_cols, block_in):
    width_in = block_in.shape[1]
    columns = [
        padded[
            time_off : time_off + n_frames, row_off : row_off + n_rows, col_off : col_off + n_cols
        ]
        for time_off in range(3)
        for row_off in range(3)
        for col_off in range(3)
    ]
    stacked = jnp.stack(columns, axis=3).reshape(n_frames * n_rows * n_cols, 27 * width_in)
    matrix = block_in.reshape(27 * width_in, block_in.shape[2])
    return jnp.dot(stacked, matrix, preferred_element_type=jnp.float32)


def body(latent, gn_gain, gn_bias, conv_weight, conv_bias):
    n_frames, n_rows, n_cols, n_chans = latent.shape
    normed = normalize(latent, gn_gain, gn_bias)
    full_feat = lax.all_gather(normed, "chan", axis=3, tiled=True)
    earlier = shifted(full_feat, "tm", 1)
    extended = jnp.concatenate([earlier, full_feat], axis=0)
    rimmed = extended_2(extended, (("tile", 2),), 1)
    padded = jnp.pad(rimmed, ((0, 0), (1, 1), (0, 0), (0, 0)))
    summed = conv_term(
        padded, n_frames, n_rows, n_cols, lax.all_gather(conv_weight, "tm", axis=1, tiled=True)
    )
    result = (summed + conv_bias.astype(jnp.float32)).astype(jnp.bfloat16)
    return result.reshape(n_frames, n_rows, n_cols, n_chans)


def near_of(s):
    return s + 1 - 2 * (s % 2)


def mid_of(s):
    return (s + 2) % 4


def far_of(s):
    return 3 - s


def three(value):
    high = value.astype(jnp.bfloat16)
    rest = value - high.astype(jnp.float32)
    mid = rest.astype(jnp.bfloat16)
    low = (rest - mid.astype(jnp.float32)).astype(jnp.bfloat16)
    return [high.astype(jnp.float32), mid.astype(jnp.float32), low.astype(jnp.float32)]


def tail_rows(rows):
    rows = jnp.concatenate(rows, axis=0)
    filler = jnp.zeros((STAT_ROWS - rows.shape[0], rows.shape[1]), jnp.float32)
    return jnp.concatenate([rows, filler], axis=0).astype(jnp.bfloat16)


def sum_rows(wide):
    total = jnp.sum(wide, axis=0, keepdims=True)
    square = jnp.sum(wide * wide, axis=0, keepdims=True)
    return three(total) + three(square)


def by_parity(fill):
    parity = lax.axis_index("tm") % 2

    @pl.when(parity == 0)
    def _():
        fill(slice(0, LANES), slice(LANES, 2 * LANES))

    @pl.when(parity == 1)
    def _():
        fill(slice(LANES, 2 * LANES), slice(0, LANES))


def cells_kernel(latent_ref, same_ref, next_ref, *, cells):
    def fill(same, following):
        for out_ref, lanes in ((same_ref, same), (next_ref, following)):
            out_ref[:cells] = latent_ref[:, lanes]
            out_ref[cells:] = tail_rows(sum_rows(latent_ref[:, lanes].astype(jnp.float32)))

    by_parity(fill)


def edges_kernel(latent_ref, gain_ref, bias_ref, same_ref, next_ref, wide_ref, *, edges, cols):
    first = jnp.where(lax.axis_index("tile") == 0, cols - 1, 0)

    def fill(same, following):
        for out_ref, lanes in ((same_ref, same), (next_ref, following)):
            wide = latent_ref[:, lanes].astype(jnp.float32)
            wide_ref[...] = wide
            out_ref[:edges] = wide_ref[pl.ds(first, edges, stride=cols), :].astype(jnp.bfloat16)
            params_rows = [ref[:, lanes].astype(jnp.float32) for ref in (gain_ref, bias_ref)]
            out_ref[edges:] = tail_rows(sum_rows(wide) + params_rows)

    by_parity(fill)


def join_kernel(*refs):
    out_ref = refs[-1]
    at = 0
    for ref in refs[:-1]:
        out_ref[at : at + ref.shape[0]] = ref[...]
        at += ref.shape[0]


def group_total(row, group_ch):
    lane = lax.broadcasted_iota(jnp.int32, row.shape, 1)
    step = 1
    while step < group_ch:
        up = pltpu.roll(row, LANES - step, 1)
        down = pltpu.roll(row, step, 1)
        row = row + jnp.where((lane // step) % 2 == 0, up, down)
        step *= 2
    return row


def spread_kernel(
    same_ref, a_ref, edge_a_ref, b_ref, edge_b_ref, swapped_ref, out_ref, own_ref,
    *, frames, rows, cols, entries, first,
):
    s = lax.axis_index("tm")
    home = lax.axis_index("chan") == s // 2
    tile = lax.axis_index("tile")
    cells = frames * rows * cols
    edges = frames * rows
    split = cells + STAT_ROWS
    height = split + edges + STAT_ROWS

    @pl.when(home)
    def _():
        own_ref[...] = same_ref[...]

    @pl.when(jnp.logical_not(home))
    def _():
        own_ref[...] = swapped_ref[height : height + split]

    near, mid, far = near_of(s), mid_of(s), far_of(s)
    pieces = (
        (own_ref, swapped_ref, height + split, jnp.where(home, s, mid)),
        (a_ref, edge_a_ref, 0, jnp.where(home, near, far)),
        (b_ref, edge_b_ref, 0, jnp.where(home, mid, s)),
        (swapped_ref, swapped_ref, split, jnp.where(home, far, near)),
    )
    stats = jnp.zeros((STAT_ROWS, LANES), jnp.float32)
    for ref, edge_ref, skip, _ in pieces:
        last = edge_ref[skip + edges : skip + edges + STAT_ROWS].astype(jnp.float32)
        stats = stats + ref[cells : cells + STAT_ROWS].astype(jnp.float32) + last
    total = group_total(stats[0:1] + stats[1:2] + stats[2:3], CH // GROUPS) / entries
    square = group_total(stats[3:4] + stats[4:5] + stats[5:6], CH // GROUPS) / entries
    scale = lax.rsqrt(square - total * total + EPS) * last[6:7]
    shift = last[7:8]

    def normed(raw):
        value = (raw.astype(jnp.float32) - total) * scale + shift
        return value / (1.0 + jnp.exp(-value))

    n_all = out_ref.shape[1]
    zero_row = jnp.zeros((cols, LANES), jnp.bfloat16)
    for d in range(3):
        for f in range(n_all):
            out_ref[d, f, 0] = zero_row
            out_ref[d, f, rows + 1] = zero_row

    def clear():
        for d in range(3):
            for f in range(2):
                out_ref[d, f, 1 : rows + 1] = jnp.zeros((rows, cols, LANES), jnp.bfloat16)

    col = lax.broadcasted_iota(jnp.int32, (rows, cols, LANES), 1)
    span = rows * cols

    def place(ref, edge_ref, skip, start, f):
        value = normed(ref[f * span : (f + 1) * span])
        edge = normed(edge_ref[skip + f * rows : skip + (f + 1) * rows])
        edge = jnp.broadcast_to(edge[:, None, :], (rows, cols, LANES))
        left = pltpu.roll(value, 1, 0).reshape(rows, cols, LANES)
        left = jnp.where(col == 0, jnp.where(tile == 1, edge, 0.0), left)
        right = pltpu.roll(value, span - 1, 0).reshape(rows, cols, LANES)
        right = jnp.where(col == cols - 1, jnp.where(tile == 0, edge, 0.0), right)
        at = start + f
        out_ref[0, at, 1 : rows + 1] = left.astype(jnp.bfloat16)
        out_ref[1, at, 1 : rows + 1] = value.reshape(rows, cols, LANES).astype(jnp.bfloat16)
        out_ref[2, at, 1 : rows + 1] = right.astype(jnp.bfloat16)

    if first:
        core = lax.axis_index("chan")
        target = jnp.where(core == 0, far, mid)
        pl.when(target == 0)(clear)
        for ref, edge_ref, skip, block in pieces:
            start = (block - target + 1) * frames
            for f in range(frames):
                at = start + f
                wanted = jnp.logical_and(at >= core, at <= core + 2)
                pl.when(wanted)(functools.partial(place, ref, edge_ref, skip, start, f))
    else:
        clear()
        for ref, edge_ref, skip, block in pieces:
            for f in range(frames):
                place(ref, edge_ref, skip, 2 + block * frames, f)


def partial_kernel(spread_ref, weight_ref, *rest, jobs, n_adds, n_outs, frames, rows, cols, with_bias):
    outs = rest[len(rest) - n_outs :]
    s = lax.axis_index("tm")
    span = rows * cols
    for frame_of, out, place, added in jobs:
        at = frame_of(s)
        stacked = jnp.concatenate(
            [
                spread_ref[d, at + a, b : b + rows].reshape(span, LANES)
                for a in range(3)
                for b in range(3)
                for d in range(3)
            ],
            axis=1,
        )
        total = jnp.dot(stacked, weight_ref[...], preferred_element_type=jnp.float32)
        for ref, core in added:
            more = rest[ref][...].astype(jnp.float32)
            total = total + (more if core is None else jnp.where(lax.axis_index("chan") == core, more, 0.0))
        if with_bias:
            total = total + rest[n_adds][...].astype(jnp.float32)
        outs[out][place * span : (place + 1) * span] = total.astype(outs[out].dtype)


def finish_kernel(whole_ref, second_ref, one_ref, other_ref, out_ref):
    del whole_ref
    total = second_ref[...] + one_ref[...].astype(jnp.float32) + other_ref[...].astype(jnp.float32)
    out_ref[...] = total.astype(out_ref.dtype)


def place_kernel(first_ref, out_ref):
    out_ref[...] = first_ref[...].astype(out_ref.dtype)


def params():
    return pltpu.CompilerParams(vmem_limit_bytes=VMEM)


def split_body(latent, gn_gain, gn_bias, conv_weight, conv_bias):
    frames, rows, cols, chans = latent.shape
    if frames != 2:
        return body(latent, gn_gain, gn_bias, conv_weight, conv_bias)
    outs = conv_weight.shape[2]
    cells = frames * rows * cols
    edges = frames * rows
    n_blocks = lax.axis_size("tm")
    entries = cells * n_blocks * lax.axis_size("tile") * (CH // GROUPS)
    flat = latent.reshape(cells, chans)

    def table(height):
        return jax.ShapeDtypeStruct((height, LANES), jnp.bfloat16)

    same, following = pl.pallas_call(
        functools.partial(cells_kernel, cells=cells),
        out_shape=(table(cells + STAT_ROWS),) * 2,
        compiler_params=params(),
    )(flat)
    edge_same, edge_following = pl.pallas_call(
        functools.partial(edges_kernel, edges=edges, cols=cols),
        out_shape=(table(edges + STAT_ROWS),) * 2,
        scratch_shapes=[pltpu.VMEM((cells, LANES), jnp.float32)],
        compiler_params=params(),
    )(flat, gn_gain.reshape(1, chans), gn_bias.reshape(1, chans))

    route_a, route_b, edge_a, edge_b = [], [], [], []
    for s in range(n_blocks):
        h = s // 2
        hops = [
            (route_a, edge_a, h, near_of(s), h),
            (route_a, edge_a, 1 - h, far_of(s), h),
            (route_b, edge_b, h, s, 1 - h),
            (route_b, edge_b, 1 - h, mid_of(s), 1 - h),
        ]
        for route, edge_route, core, there, core_there in hops:
            route.append((2 * s + core, 2 * there + core_there))
            for x in range(2):
                edge_route.append((4 * s + 2 * x + core, 4 * there + 2 * (1 - x) + core_there))
    swap = [(0, 1), (1, 0)]
    both = ("tm", "chan")
    got_b = lax.ppermute(same, both, route_b)
    got_a = lax.ppermute(following, both, route_a)
    got_edge_b = lax.ppermute(edge_same, ("tm", "tile", "chan"), edge_b)
    got_edge_a = lax.ppermute(edge_following, ("tm", "tile", "chan"), edge_a)

    received = (got_a, got_edge_a, got_b, got_edge_b)
    joined = pl.pallas_call(
        join_kernel,
        out_shape=table(sum(part.shape[0] for part in received)),
        compiler_params=params(),
    )(*received)
    swapped = lax.ppermute(joined, "chan", swap)

    def spread_out(n_frames, first, after=None):
        head = same if after is None else lax.optimization_barrier((same, after))[0]
        return pl.pallas_call(
            functools.partial(
                spread_kernel, frames=frames, rows=rows, cols=cols, entries=entries, first=first
            ),
            out_shape=jax.ShapeDtypeStruct((3, n_frames, rows + 2, cols, LANES), jnp.bfloat16),
            scratch_shapes=[pltpu.VMEM(same.shape, jnp.bfloat16)],
            compiler_params=params(),
        )(head, *received, swapped)

    narrow = spread_out(2 + frames, True)

    weight = conv_weight.reshape(27 * LANES, outs)
    bias = conv_bias.reshape(1, outs)

    def partial_sums(acts, jobs, spans, adds=(), with_bias=False, dtype=jnp.bfloat16, after=None, cost=1):
        source = acts if after is None else lax.optimization_barrier((acts, after))[0]
        return pl.pallas_call(
            functools.partial(
                partial_kernel,
                jobs=jobs,
                n_adds=len(adds),
                n_outs=len(spans),
                frames=frames,
                rows=rows,
                cols=cols,
                with_bias=with_bias,
            ),
            out_shape=[jax.ShapeDtypeStruct((n * rows * cols, outs), dtype) for n in spans],
            compiler_params=params(),
            cost_estimate=pl.CostEstimate(flops=cost, transcendentals=0, bytes_accessed=1),
        )(source, weight, *adds, *([bias] if with_bias else []))

    def mixed(core, ours, theirs):
        return lambda s: jnp.where(lax.axis_index("chan") == core, ours(s), theirs(s))

    def frame(block_of, f):
        return lambda s: block_of(s) * frames + f

    def route(core, goal):
        return [
            (2 * s + c, 2 * (goal(s) if c == core else near_of(s)) + c)
            for s in range(n_blocks)
            for c in range(2)
        ]

    lead = partial_sums(narrow, [(mixed(0, lambda s: 0, lambda s: 1), 0, 0, ())], [1], cost=1 << 32)
    spread = spread_out(2 + n_blocks * frames, False, lead[0])
    second = mixed(1, frame(far_of, 0), frame(mid_of, 1))
    second = partial_sums(spread, [(second, 0, 0, ())], [1], after=lead, cost=1 << 32)
    jobs = [(mixed(core, frame(mid_of, 0), frame(near_of, 0)), core, 0, ()) for core in range(2)]
    straight = partial_sums(spread, jobs, [1, 1], after=second, cost=1 << 32)
    got_1 = lax.ppermute(lead[0], both, route(0, far_of))
    got_2 = lax.ppermute(second[0], both, route(1, far_of))
    got_3 = lax.ppermute(straight[0], both, route(0, mid_of))
    got_4 = lax.ppermute(straight[1], both, route(1, mid_of))
    last = [
        partial_sums(
            spread, [(mixed(core, frame(far_of, 1), frame(near_of, 1)), 0, 0, ((0, core),))], [1], (got,), after=after
        )[0]
        for core, got, after in ((0, got_2, straight), (1, got_1, got_2))
    ]
    got_5, got_6 = [lax.ppermute(sent, both, route(core, far_of)) for core, sent in enumerate(last)]
    home = []
    for f, adds, added in (
        (0, (got_1, got_2, got_3, got_4), ((0, 0), (1, 1), (2, None), (3, None))),
        (1, (), ()),
    ):
        jobs = [(frame(lambda s: s, f), 0, 0, added)]
        after = home or None
        home += partial_sums(spread, jobs, [1], adds, True, jnp.float32, after=after, cost=1 << 35)
    span = rows * cols
    whole = pl.pallas_call(
        place_kernel,
        grid=(1,),
        in_specs=[pl.BlockSpec((span, outs), lambda i: (0, 0))],
        out_specs=pl.BlockSpec((span, outs), lambda i: (0, 0)),
        out_shape=jax.ShapeDtypeStruct((cells, outs), jnp.bfloat16),
        compiler_params=params(),
    )(home[0])
    result = pl.pallas_call(
        finish_kernel,
        grid=(1,),
        in_specs=[pl.BlockSpec(memory_space=pl.ANY)] + [pl.BlockSpec((span, outs), lambda i: (0, 0))] * 3,
        out_specs=pl.BlockSpec((span, outs), lambda i: (1, 0)),
        out_shape=jax.ShapeDtypeStruct((cells, outs), jnp.bfloat16),
        input_output_aliases={0: 0},
        compiler_params=params(),
    )(whole, home[1], got_5, got_6)
    return result.reshape(frames, rows, cols, outs)


def splits(mesh):
    size = mesh.shape
    return size["tm"] == 4 and size["tile"] == 2 and size["chan"] == 2 and CH == size["tm"] * LANES


def solution(mesh):
    in_specs = (
        P(("groups", "tm"), None, "tile", "chan"),
        P("chan"),
        P("chan"),
        P(None, "tm", "chan"),
        P("chan"),
    )
    out_specs = P(("groups", "tm"), None, "tile", "chan")
    chosen = split_body if splits(mesh) else body
    return jax.shard_map(chosen, mesh=mesh, in_specs=in_specs, out_specs=out_specs, check_vma=False)
```

```python
import functools

import jax
import jax.numpy as jnp
from jax import lax
from jax.experimental import pallas as pl
from jax.experimental.pallas import tpu as pltpu
from jax.sharding import PartitionSpec as P

CH = 512
GROUPS = 32
EPS = 1e-06
LANES = 128
VMEM = 24 << 20
STAT_ROWS = 16


def shifted(block, axis, distance):
    devices = range(lax.axis_size(axis))
    route = [(i - distance, i) for i in devices if i - distance in devices]
    return lax.ppermute(block, axis, route)


def extended_2(cells, sides, width):
    for axis, dim in sides:
        count = lax.axis_size(axis)
        ends = count - 1
        head = lax.slice_in_dim(cells, 0, width, axis=dim)
        tail = lax.slice_in_dim(cells, cells.shape[dim] - width, cells.shape[dim], axis=dim)
        cells = jnp.concatenate(
            [
                lax.ppermute(tail, axis, [(i, (i + 1) % count) for i in range(ends)]),
                cells,
                lax.ppermute(head, axis, [((i + 1) % count, i) for i in range(ends)]),
            ],
            axis=dim,
        )
    return cells


def normalize(latent, gn_gain, gn_bias):
    values = latent.astype(jnp.float32)
    n_frames, n_rows, n_cols, n_chans = latent.shape
    group_ch = CH // GROUPS
    local_groups = n_chans // group_ch
    shaped = values.reshape(n_frames, n_rows, n_cols, local_groups, group_ch)
    part_sum = jnp.sum(shaped, axis=(0, 1, 2, 4))
    part_square = jnp.sum(shaped * shaped, axis=(0, 1, 2, 4))
    total_sum, total_square = lax.psum((part_sum, part_square), ("tm", "tile"))
    entries = n_frames * n_rows * n_cols * group_ch * lax.axis_size("tm") * lax.axis_size("tile")
    mean_grp = total_sum / entries
    square_grp = total_square / entries
    inv_grp = lax.rsqrt(square_grp - mean_grp * mean_grp + 1e-06)
    mean_ch = jnp.repeat(mean_grp, group_ch)
    inv_ch = jnp.repeat(inv_grp, group_ch)
    scaled = (values - mean_ch) * inv_ch * gn_gain.astype(jnp.float32) + gn_bias.astype(jnp.float32)
    return jax.nn.silu(scaled).astype(jnp.bfloat16)


def conv_term(padded, n_frames, n_rows, n_cols, block_in):
    width_in = block_in.shape[1]
    columns = [
        padded[
            time_off : time_off + n_frames, row_off : row_off + n_rows, col_off : col_off + n_cols
        ]
        for time_off in range(3)
        for row_off in range(3)
        for col_off in range(3)
    ]
    stacked = jnp.stack(columns, axis=3).reshape(n_frames * n_rows * n_cols, 27 * width_in)
    matrix = block_in.reshape(27 * width_in, block_in.shape[2])
    return jnp.dot(stacked, matrix, preferred_element_type=jnp.float32)


def body(latent, gn_gain, gn_bias, conv_weight, conv_bias):
    n_frames, n_rows, n_cols, n_chans = latent.shape
    normed = normalize(latent, gn_gain, gn_bias)
    full_feat = lax.all_gather(normed, "chan", axis=3, tiled=True)
    earlier = shifted(full_feat, "tm", 1)
    extended = jnp.concatenate([earlier, full_feat], axis=0)
    rimmed = extended_2(extended, (("tile", 2),), 1)
    padded = jnp.pad(rimmed, ((0, 0), (1, 1), (0, 0), (0, 0)))
    summed = conv_term(
        padded, n_frames, n_rows, n_cols, lax.all_gather(conv_weight, "tm", axis=1, tiled=True)
    )
    result = (summed + conv_bias.astype(jnp.float32)).astype(jnp.bfloat16)
    return result.reshape(n_frames, n_rows, n_cols, n_chans)


def near_of(s):
    return s + 1 - 2 * (s % 2)


def mid_of(s):
    return (s + 2) % 4


def far_of(s):
    return 3 - s


def three(value):
    high = value.astype(jnp.bfloat16)
    rest = value - high.astype(jnp.float32)
    mid = rest.astype(jnp.bfloat16)
    low = (rest - mid.astype(jnp.float32)).astype(jnp.bfloat16)
    return [high.astype(jnp.float32), mid.astype(jnp.float32), low.astype(jnp.float32)]


def tail_rows(rows):
    rows = jnp.concatenate(rows, axis=0)
    filler = jnp.zeros((STAT_ROWS - rows.shape[0], rows.shape[1]), jnp.float32)
    return jnp.concatenate([rows, filler], axis=0).astype(jnp.bfloat16)


def sum_rows(wide):
    total = jnp.sum(wide, axis=0, keepdims=True)
    square = jnp.sum(wide * wide, axis=0, keepdims=True)
    return three(total) + three(square)


def by_parity(fill):
    parity = lax.axis_index("tm") % 2

    @pl.when(parity == 0)
    def _():
        fill(slice(0, LANES), slice(LANES, 2 * LANES))

    @pl.when(parity == 1)
    def _():
        fill(slice(LANES, 2 * LANES), slice(0, LANES))


def cells_kernel(latent_ref, same_ref, next_ref, *, cells):
    def fill(same, following):
        for out_ref, lanes in ((same_ref, same), (next_ref, following)):
            out_ref[:cells] = latent_ref[:, lanes]
            out_ref[cells:] = tail_rows(sum_rows(latent_ref[:, lanes].astype(jnp.float32)))

    by_parity(fill)


def edges_kernel(latent_ref, gain_ref, bias_ref, same_ref, next_ref, wide_ref, *, edges, cols):
    first = jnp.where(lax.axis_index("tile") == 0, cols - 1, 0)

    def fill(same, following):
        for out_ref, lanes in ((same_ref, same), (next_ref, following)):
            wide = latent_ref[:, lanes].astype(jnp.float32)
            wide_ref[...] = wide
            out_ref[:edges] = wide_ref[pl.ds(first, edges, stride=cols), :].astype(jnp.bfloat16)
            params_rows = [ref[:, lanes].astype(jnp.float32) for ref in (gain_ref, bias_ref)]
            out_ref[edges:] = tail_rows(sum_rows(wide) + params_rows)

    by_parity(fill)


def join_kernel(*refs):
    out_ref = refs[-1]
    at = 0
    for ref in refs[:-1]:
        out_ref[at : at + ref.shape[0]] = ref[...]
        at += ref.shape[0]


def group_total(row, group_ch):
    lane = lax.broadcasted_iota(jnp.int32, row.shape, 1)
    step = 1
    while step < group_ch:
        up = pltpu.roll(row, LANES - step, 1)
        down = pltpu.roll(row, step, 1)
        row = row + jnp.where((lane // step) % 2 == 0, up, down)
        step *= 2
    return row


def spread_kernel(
    same_ref, a_ref, edge_a_ref, b_ref, edge_b_ref, swapped_ref, out_ref, own_ref,
    *, frames, rows, cols, entries, first,
):
    s = lax.axis_index("tm")
    home = lax.axis_index("chan") == s // 2
    tile = lax.axis_index("tile")
    cells = frames * rows * cols
    edges = frames * rows
    split = cells + STAT_ROWS
    height = split + edges + STAT_ROWS

    @pl.when(home)
    def _():
        own_ref[...] = same_ref[...]

    @pl.when(jnp.logical_not(home))
    def _():
        own_ref[...] = swapped_ref[height : height + split]

    near, mid, far = near_of(s), mid_of(s), far_of(s)
    pieces = (
        (own_ref, swapped_ref, height + split, jnp.where(home, s, mid)),
        (a_ref, edge_a_ref, 0, jnp.where(home, near, far)),
        (b_ref, edge_b_ref, 0, jnp.where(home, mid, s)),
        (swapped_ref, swapped_ref, split, jnp.where(home, far, near)),
    )
    stats = jnp.zeros((STAT_ROWS, LANES), jnp.float32)
    for ref, edge_ref, skip, _ in pieces:
        last = edge_ref[skip + edges : skip + edges + STAT_ROWS].astype(jnp.float32)
        stats = stats + ref[cells : cells + STAT_ROWS].astype(jnp.float32) + last
    total = group_total(stats[0:1] + stats[1:2] + stats[2:3], CH // GROUPS) / entries
    square = group_total(stats[3:4] + stats[4:5] + stats[5:6], CH // GROUPS) / entries
    scale = lax.rsqrt(square - total * total + EPS) * last[6:7]
    shift = last[7:8]

    def normed(raw):
        value = (raw.astype(jnp.float32) - total) * scale + shift
        return value / (1.0 + jnp.exp(-value))

    n_all = out_ref.shape[1]
    zero_row = jnp.zeros((cols, LANES), jnp.bfloat16)
    for d in range(3):
        for f in range(n_all):
            out_ref[d, f, 0] = zero_row
            out_ref[d, f, rows + 1] = zero_row

    def clear():
        for d in range(3):
            for f in range(2):
                out_ref[d, f, 1 : rows + 1] = jnp.zeros((rows, cols, LANES), jnp.bfloat16)

    col = lax.broadcasted_iota(jnp.int32, (rows, cols, LANES), 1)
    span = rows * cols

    def place(ref, edge_ref, skip, start, f):
        value = normed(ref[f * span : (f + 1) * span])
        edge = normed(edge_ref[skip + f * rows : skip + (f + 1) * rows])
        edge = jnp.broadcast_to(edge[:, None, :], (rows, cols, LANES))
        left = pltpu.roll(value, 1, 0).reshape(rows, cols, LANES)
        left = jnp.where(col == 0, jnp.where(tile == 1, edge, 0.0), left)
        right = pltpu.roll(value, span - 1, 0).reshape(rows, cols, LANES)
        right = jnp.where(col == cols - 1, jnp.where(tile == 0, edge, 0.0), right)
        at = start + f
        out_ref[0, at, 1 : rows + 1] = left.astype(jnp.bfloat16)
        out_ref[1, at, 1 : rows + 1] = value.reshape(rows, cols, LANES).astype(jnp.bfloat16)
        out_ref[2, at, 1 : rows + 1] = right.astype(jnp.bfloat16)

    if first:
        core = lax.axis_index("chan")
        target = jnp.where(core == 0, far, mid)
        pl.when(target == 0)(clear)
        for ref, edge_ref, skip, block in pieces:
            start = (block - target + 1) * frames
            for f in range(frames):
                at = start + f
                wanted = jnp.logical_and(at >= core, at <= core + 2)
                pl.when(wanted)(functools.partial(place, ref, edge_ref, skip, start, f))
    else:
        clear()
        for ref, edge_ref, skip, block in pieces:
            for f in range(frames):
                place(ref, edge_ref, skip, 2 + block * frames, f)


def partial_kernel(spread_ref, weight_ref, *rest, jobs, n_adds, n_outs, frames, rows, cols, with_bias):
    outs = rest[len(rest) - n_outs :]
    s = lax.axis_index("tm")
    span = rows * cols
    for frame_of, out, place, added in jobs:
        at = frame_of(s)
        stacked = jnp.concatenate(
            [
                spread_ref[d, at + a, b : b + rows].reshape(span, LANES)
                for a in range(3)
                for b in range(3)
                for d in range(3)
            ],
            axis=1,
        )
        total = jnp.dot(stacked, weight_ref[...], preferred_element_type=jnp.float32)
        for ref, core in added:
            more = rest[ref][...].astype(jnp.float32)
            total = total + (more if core is None else jnp.where(lax.axis_index("chan") == core, more, 0.0))
        if with_bias:
            total = total + rest[n_adds][...].astype(jnp.float32)
        outs[out][place * span : (place + 1) * span] = total.astype(outs[out].dtype)


def finish_kernel(whole_ref, second_ref, one_ref, other_ref, out_ref):
    del whole_ref
    total = second_ref[...] + one_ref[...].astype(jnp.float32) + other_ref[...].astype(jnp.float32)
    out_ref[...] = total.astype(out_ref.dtype)


def place_kernel(first_ref, out_ref):
    out_ref[...] = first_ref[...].astype(out_ref.dtype)


def params():
    return pltpu.CompilerParams(vmem_limit_bytes=VMEM)


def split_body(latent, gn_gain, gn_bias, conv_weight, conv_bias):
    frames, rows, cols, chans = latent.shape
    if frames != 2:
        return body(latent, gn_gain, gn_bias, conv_weight, conv_bias)
    outs = conv_weight.shape[2]
    cells = frames * rows * cols
    edges = frames * rows
    n_blocks = lax.axis_size("tm")
    entries = cells * n_blocks * lax.axis_size("tile") * (CH // GROUPS)
    flat = latent.reshape(cells, chans)

    def table(height):
        return jax.ShapeDtypeStruct((height, LANES), jnp.bfloat16)

    same, following = pl.pallas_call(
        functools.partial(cells_kernel, cells=cells),
        out_shape=(table(cells + STAT_ROWS),) * 2,
        compiler_params=params(),
    )(flat)
    edge_same, edge_following = pl.pallas_call(
        functools.partial(edges_kernel, edges=edges, cols=cols),
        out_shape=(table(edges + STAT_ROWS),) * 2,
        scratch_shapes=[pltpu.VMEM((cells, LANES), jnp.float32)],
        compiler_params=params(),
    )(flat, gn_gain.reshape(1, chans), gn_bias.reshape(1, chans))

    route_a, route_b, edge_a, edge_b = [], [], [], []
    for s in range(n_blocks):
        h = s // 2
        hops = [
            (route_a, edge_a, h, near_of(s), h),
            (route_a, edge_a, 1 - h, far_of(s), h),
            (route_b, edge_b, h, s, 1 - h),
            (route_b, edge_b, 1 - h, mid_of(s), 1 - h),
        ]
        for route, edge_route, core, there, core_there in hops:
            route.append((2 * s + core, 2 * there + core_there))
            for x in range(2):
                edge_route.append((4 * s + 2 * x + core, 4 * there + 2 * (1 - x) + core_there))
    swap = [(0, 1), (1, 0)]
    both = ("tm", "chan")
    got_b = lax.ppermute(same, both, route_b)
    got_a = lax.ppermute(following, both, route_a)
    got_edge_b = lax.ppermute(edge_same, ("tm", "tile", "chan"), edge_b)
    got_edge_a = lax.ppermute(edge_following, ("tm", "tile", "chan"), edge_a)

    received = (got_a, got_edge_a, got_b, got_edge_b)
    joined = pl.pallas_call(
        join_kernel,
        out_shape=table(sum(part.shape[0] for part in received)),
        compiler_params=params(),
    )(*received)
    swapped = lax.ppermute(joined, "chan", swap)

    def spread_out(n_frames, first, after=None):
        head = same if after is None else lax.optimization_barrier((same, after))[0]
        return pl.pallas_call(
            functools.partial(
                spread_kernel, frames=frames, rows=rows, cols=cols, entries=entries, first=first
            ),
            out_shape=jax.ShapeDtypeStruct((3, n_frames, rows + 2, cols, LANES), jnp.bfloat16),
            scratch_shapes=[pltpu.VMEM(same.shape, jnp.bfloat16)],
            compiler_params=params(),
        )(head, *received, swapped)

    narrow = spread_out(2 + frames, True)

    weight = conv_weight.reshape(27 * LANES, outs)
    bias = conv_bias.reshape(1, outs)

    def partial_sums(acts, jobs, spans, adds=(), with_bias=False, dtype=jnp.bfloat16, after=None, cost=1):
        source = acts if after is None else lax.optimization_barrier((acts, after))[0]
        return pl.pallas_call(
            functools.partial(
                partial_kernel,
                jobs=jobs,
                n_adds=len(adds),
                n_outs=len(spans),
                frames=frames,
                rows=rows,
                cols=cols,
                with_bias=with_bias,
            ),
            out_shape=[jax.ShapeDtypeStruct((n * rows * cols, outs), dtype) for n in spans],
            compiler_params=params(),
            cost_estimate=pl.CostEstimate(flops=cost, transcendentals=0, bytes_accessed=1),
        )(source, weight, *adds, *([bias] if with_bias else []))

    def mixed(core, ours, theirs):
        return lambda s: jnp.where(lax.axis_index("chan") == core, ours(s), theirs(s))

    def frame(block_of, f):
        return lambda s: block_of(s) * frames + f

    def route(core, goal):
        return [
            (2 * s + c, 2 * (goal(s) if c == core else near_of(s)) + c)
            for s in range(n_blocks)
            for c in range(2)
        ]

    lead = partial_sums(narrow, [(mixed(0, lambda s: 0, lambda s: 1), 0, 0, ())], [1], cost=1 << 32)
    spread = spread_out(2 + n_blocks * frames, False, lead[0])
    second = mixed(1, frame(far_of, 0), frame(mid_of, 1))
    second = partial_sums(spread, [(second, 0, 0, ())], [1], after=lead, cost=1 << 32)
    jobs = [(mixed(core, frame(mid_of, 0), frame(near_of, 0)), core, 0, ()) for core in range(2)]
    straight = partial_sums(spread, jobs, [1, 1], after=second, cost=1 << 32)
    got_1 = lax.ppermute(lead[0], both, route(0, far_of))
    got_2 = lax.ppermute(second[0], both, route(1, far_of))
    got_3 = lax.ppermute(straight[0], both, route(0, mid_of))
    got_4 = lax.ppermute(straight[1], both, route(1, mid_of))
    last = [
        partial_sums(
            spread, [(mixed(core, frame(far_of, 1), frame(near_of, 1)), 0, 0, ((0, core),))], [1], (got,), after=after
        )[0]
        for core, got, after in ((1, got_1, straight), (0, got_2, got_1))
    ]
    got_5, got_6 = [lax.ppermute(sent, both, route(1 - core, far_of)) for core, sent in enumerate(last)]
    home = []
    for f, adds, added in (
        (0, (got_1, got_2, got_3, got_4), ((0, 0), (1, 1), (2, None), (3, None))),
        (1, (), ()),
    ):
        jobs = [(frame(lambda s: s, f), 0, 0, added)]
        after = home or None
        home += partial_sums(spread, jobs, [1], adds, True, jnp.float32, after=after, cost=1 << 35)
    span = rows * cols
    whole = pl.pallas_call(
        place_kernel,
        grid=(1,),
        in_specs=[pl.BlockSpec((span, outs), lambda i: (0, 0))],
        out_specs=pl.BlockSpec((span, outs), lambda i: (0, 0)),
        out_shape=jax.ShapeDtypeStruct((cells, outs), jnp.bfloat16),
        compiler_params=params(),
    )(home[0])
    result = pl.pallas_call(
        finish_kernel,
        grid=(1,),
        in_specs=[pl.BlockSpec(memory_space=pl.ANY)] + [pl.BlockSpec((span, outs), lambda i: (0, 0))] * 3,
        out_specs=pl.BlockSpec((span, outs), lambda i: (1, 0)),
        out_shape=jax.ShapeDtypeStruct((cells, outs), jnp.bfloat16),
        input_output_aliases={0: 0},
        compiler_params=params(),
    )(whole, home[1], got_5, got_6)
    return result.reshape(frames, rows, cols, outs)


def splits(mesh):
    size = mesh.shape
    return size["tm"] == 4 and size["tile"] == 2 and size["chan"] == 2 and CH == size["tm"] * LANES


def solution(mesh):
    in_specs = (
        P(("groups", "tm"), None, "tile", "chan"),
        P("chan"),
        P("chan"),
        P(None, "tm", "chan"),
        P("chan"),
    )
    out_specs = P(("groups", "tm"), None, "tile", "chan")
    chosen = split_body if splits(mesh) else body
    return jax.shard_map(chosen, mesh=mesh, in_specs=in_specs, out_specs=out_specs, check_vma=False)
```

```python
import functools

import jax
import jax.numpy as jnp
from jax import lax
from jax.experimental import pallas as pl
from jax.experimental.pallas import tpu as pltpu
from jax.sharding import PartitionSpec as P

CH = 512
GROUPS = 32
EPS = 1e-06
LANES = 128
VMEM = 24 << 20
STAT_ROWS = 16


def shifted(block, axis, distance):
    devices = range(lax.axis_size(axis))
    route = [(i - distance, i) for i in devices if i - distance in devices]
    return lax.ppermute(block, axis, route)


def extended_2(cells, sides, width):
    for axis, dim in sides:
        count = lax.axis_size(axis)
        ends = count - 1
        head = lax.slice_in_dim(cells, 0, width, axis=dim)
        tail = lax.slice_in_dim(cells, cells.shape[dim] - width, cells.shape[dim], axis=dim)
        cells = jnp.concatenate(
            [
                lax.ppermute(tail, axis, [(i, (i + 1) % count) for i in range(ends)]),
                cells,
                lax.ppermute(head, axis, [((i + 1) % count, i) for i in range(ends)]),
            ],
            axis=dim,
        )
    return cells


def normalize(latent, gn_gain, gn_bias):
    values = latent.astype(jnp.float32)
    n_frames, n_rows, n_cols, n_chans = latent.shape
    group_ch = CH // GROUPS
    local_groups = n_chans // group_ch
    shaped = values.reshape(n_frames, n_rows, n_cols, local_groups, group_ch)
    part_sum = jnp.sum(shaped, axis=(0, 1, 2, 4))
    part_square = jnp.sum(shaped * shaped, axis=(0, 1, 2, 4))
    total_sum, total_square = lax.psum((part_sum, part_square), ("tm", "tile"))
    entries = n_frames * n_rows * n_cols * group_ch * lax.axis_size("tm") * lax.axis_size("tile")
    mean_grp = total_sum / entries
    square_grp = total_square / entries
    inv_grp = lax.rsqrt(square_grp - mean_grp * mean_grp + 1e-06)
    mean_ch = jnp.repeat(mean_grp, group_ch)
    inv_ch = jnp.repeat(inv_grp, group_ch)
    scaled = (values - mean_ch) * inv_ch * gn_gain.astype(jnp.float32) + gn_bias.astype(jnp.float32)
    return jax.nn.silu(scaled).astype(jnp.bfloat16)


def conv_term(padded, n_frames, n_rows, n_cols, block_in):
    width_in = block_in.shape[1]
    columns = [
        padded[
            time_off : time_off + n_frames, row_off : row_off + n_rows, col_off : col_off + n_cols
        ]
        for time_off in range(3)
        for row_off in range(3)
        for col_off in range(3)
    ]
    stacked = jnp.stack(columns, axis=3).reshape(n_frames * n_rows * n_cols, 27 * width_in)
    matrix = block_in.reshape(27 * width_in, block_in.shape[2])
    return jnp.dot(stacked, matrix, preferred_element_type=jnp.float32)


def body(latent, gn_gain, gn_bias, conv_weight, conv_bias):
    n_frames, n_rows, n_cols, n_chans = latent.shape
    normed = normalize(latent, gn_gain, gn_bias)
    full_feat = lax.all_gather(normed, "chan", axis=3, tiled=True)
    earlier = shifted(full_feat, "tm", 1)
    extended = jnp.concatenate([earlier, full_feat], axis=0)
    rimmed = extended_2(extended, (("tile", 2),), 1)
    padded = jnp.pad(rimmed, ((0, 0), (1, 1), (0, 0), (0, 0)))
    summed = conv_term(
        padded, n_frames, n_rows, n_cols, lax.all_gather(conv_weight, "tm", axis=1, tiled=True)
    )
    result = (summed + conv_bias.astype(jnp.float32)).astype(jnp.bfloat16)
    return result.reshape(n_frames, n_rows, n_cols, n_chans)


def near_of(s):
    return s + 1 - 2 * (s % 2)


def mid_of(s):
    return (s + 2) % 4


def far_of(s):
    return 3 - s


def three(value):
    high = value.astype(jnp.bfloat16)
    rest = value - high.astype(jnp.float32)
    mid = rest.astype(jnp.bfloat16)
    low = (rest - mid.astype(jnp.float32)).astype(jnp.bfloat16)
    return [high.astype(jnp.float32), mid.astype(jnp.float32), low.astype(jnp.float32)]


def tail_rows(rows):
    rows = jnp.concatenate(rows, axis=0)
    filler = jnp.zeros((STAT_ROWS - rows.shape[0], rows.shape[1]), jnp.float32)
    return jnp.concatenate([rows, filler], axis=0).astype(jnp.bfloat16)


def sum_rows(wide):
    total = jnp.sum(wide, axis=0, keepdims=True)
    square = jnp.sum(wide * wide, axis=0, keepdims=True)
    return three(total) + three(square)


def by_parity(fill):
    parity = lax.axis_index("tm") % 2

    @pl.when(parity == 0)
    def _():
        fill(slice(0, LANES), slice(LANES, 2 * LANES))

    @pl.when(parity == 1)
    def _():
        fill(slice(LANES, 2 * LANES), slice(0, LANES))


def cells_kernel(latent_ref, same_ref, next_ref, *, cells):
    def fill(same, following):
        for out_ref, lanes in ((same_ref, same), (next_ref, following)):
            out_ref[:cells] = latent_ref[:, lanes]
            out_ref[cells:] = tail_rows(sum_rows(latent_ref[:, lanes].astype(jnp.float32)))

    by_parity(fill)


def edges_kernel(latent_ref, gain_ref, bias_ref, same_ref, next_ref, wide_ref, *, edges, cols):
    first = jnp.where(lax.axis_index("tile") == 0, cols - 1, 0)

    def fill(same, following):
        for out_ref, lanes in ((same_ref, same), (next_ref, following)):
            wide = latent_ref[:, lanes].astype(jnp.float32)
            wide_ref[...] = wide
            out_ref[:edges] = wide_ref[pl.ds(first, edges, stride=cols), :].astype(jnp.bfloat16)
            params_rows = [ref[:, lanes].astype(jnp.float32) for ref in (gain_ref, bias_ref)]
            out_ref[edges:] = tail_rows(sum_rows(wide) + params_rows)

    by_parity(fill)


def join_kernel(*refs):
    out_ref = refs[-1]
    at = 0
    for ref in refs[:-1]:
        out_ref[at : at + ref.shape[0]] = ref[...]
        at += ref.shape[0]


def group_total(row, group_ch):
    lane = lax.broadcasted_iota(jnp.int32, row.shape, 1)
    step = 1
    while step < group_ch:
        up = pltpu.roll(row, LANES - step, 1)
        down = pltpu.roll(row, step, 1)
        row = row + jnp.where((lane // step) % 2 == 0, up, down)
        step *= 2
    return row


def spread_kernel(
    same_ref, a_ref, edge_a_ref, b_ref, edge_b_ref, swapped_ref, out_ref, own_ref,
    *, frames, rows, cols, entries, first,
):
    s = lax.axis_index("tm")
    home = lax.axis_index("chan") == s // 2
    tile = lax.axis_index("tile")
    cells = frames * rows * cols
    edges = frames * rows
    split = cells + STAT_ROWS
    height = split + edges + STAT_ROWS

    @pl.when(home)
    def _():
        own_ref[...] = same_ref[...]

    @pl.when(jnp.logical_not(home))
    def _():
        own_ref[...] = swapped_ref[height : height + split]

    near, mid, far = near_of(s), mid_of(s), far_of(s)
    pieces = (
        (own_ref, swapped_ref, height + split, jnp.where(home, s, mid)),
        (a_ref, edge_a_ref, 0, jnp.where(home, near, far)),
        (b_ref, edge_b_ref, 0, jnp.where(home, mid, s)),
        (swapped_ref, swapped_ref, split, jnp.where(home, far, near)),
    )
    stats = jnp.zeros((STAT_ROWS, LANES), jnp.float32)
    for ref, edge_ref, skip, _ in pieces:
        last = edge_ref[skip + edges : skip + edges + STAT_ROWS].astype(jnp.float32)
        stats = stats + ref[cells : cells + STAT_ROWS].astype(jnp.float32) + last
    total = group_total(stats[0:1] + stats[1:2] + stats[2:3], CH // GROUPS) / entries
    square = group_total(stats[3:4] + stats[4:5] + stats[5:6], CH // GROUPS) / entries
    scale = lax.rsqrt(square - total * total + EPS) * last[6:7]
    shift = last[7:8]

    def normed(raw):
        value = (raw.astype(jnp.float32) - total) * scale + shift
        half = 0.5 * value
        return half + half * jnp.tanh(half)

    n_all = out_ref.shape[1]
    zero_row = jnp.zeros((cols, LANES), jnp.bfloat16)
    for d in range(3):
        for f in range(n_all):
            out_ref[d, f, 0] = zero_row
            out_ref[d, f, rows + 1] = zero_row

    def clear():
        for d in range(3):
            for f in range(2):
                out_ref[d, f, 1 : rows + 1] = jnp.zeros((rows, cols, LANES), jnp.bfloat16)

    col = lax.broadcasted_iota(jnp.int32, (rows, cols, LANES), 1)
    span = rows * cols

    def place(ref, edge_ref, skip, start, f):
        value = normed(ref[f * span : (f + 1) * span])
        edge = normed(edge_ref[skip + f * rows : skip + (f + 1) * rows])
        edge = jnp.broadcast_to(edge[:, None, :], (rows, cols, LANES))
        left = pltpu.roll(value, 1, 0).reshape(rows, cols, LANES)
        left = jnp.where(col == 0, jnp.where(tile == 1, edge, 0.0), left)
        right = pltpu.roll(value, span - 1, 0).reshape(rows, cols, LANES)
        right = jnp.where(col == cols - 1, jnp.where(tile == 0, edge, 0.0), right)
        at = start + f
        out_ref[0, at, 1 : rows + 1] = left.astype(jnp.bfloat16)
        out_ref[1, at, 1 : rows + 1] = value.reshape(rows, cols, LANES).astype(jnp.bfloat16)
        out_ref[2, at, 1 : rows + 1] = right.astype(jnp.bfloat16)

    if first:
        core = lax.axis_index("chan")
        target = jnp.where(core == 0, far, mid)
        pl.when(target == 0)(clear)
        for ref, edge_ref, skip, block in pieces:
            start = (block - target + 1) * frames
            for f in range(frames):
                at = start + f
                wanted = jnp.logical_and(at >= core, at <= core + 2)
                pl.when(wanted)(functools.partial(place, ref, edge_ref, skip, start, f))
    else:
        clear()
        for ref, edge_ref, skip, block in pieces:
            for f in range(frames):
                place(ref, edge_ref, skip, 2 + block * frames, f)


def partial_kernel(spread_ref, weight_ref, *rest, jobs, n_adds, n_outs, frames, rows, cols, with_bias):
    outs = rest[len(rest) - n_outs :]
    s = lax.axis_index("tm")
    span = rows * cols
    for frame_of, out, place, added in jobs:
        at = frame_of(s)
        stacked = jnp.concatenate(
            [
                spread_ref[d, at + a, b : b + rows].reshape(span, LANES)
                for a in range(3)
                for b in range(3)
                for d in range(3)
            ],
            axis=1,
        )
        total = jnp.dot(stacked, weight_ref[...], preferred_element_type=jnp.float32)
        for ref, core in added:
            more = rest[ref][...].astype(jnp.float32)
            total = total + (more if core is None else jnp.where(lax.axis_index("chan") == core, more, 0.0))
        if with_bias:
            total = total + rest[n_adds][...].astype(jnp.float32)
        outs[out][place * span : (place + 1) * span] = total.astype(outs[out].dtype)


def finish_kernel(whole_ref, second_ref, one_ref, other_ref, out_ref):
    del whole_ref
    total = second_ref[...] + one_ref[...].astype(jnp.float32) + other_ref[...].astype(jnp.float32)
    out_ref[...] = total.astype(out_ref.dtype)


def place_kernel(first_ref, out_ref):
    out_ref[...] = first_ref[...].astype(out_ref.dtype)


def params():
    return pltpu.CompilerParams(vmem_limit_bytes=VMEM)


def split_body(latent, gn_gain, gn_bias, conv_weight, conv_bias):
    frames, rows, cols, chans = latent.shape
    if frames != 2:
        return body(latent, gn_gain, gn_bias, conv_weight, conv_bias)
    outs = conv_weight.shape[2]
    cells = frames * rows * cols
    edges = frames * rows
    n_blocks = lax.axis_size("tm")
    entries = cells * n_blocks * lax.axis_size("tile") * (CH // GROUPS)
    flat = latent.reshape(cells, chans)

    def table(height):
        return jax.ShapeDtypeStruct((height, LANES), jnp.bfloat16)

    same, following = pl.pallas_call(
        functools.partial(cells_kernel, cells=cells),
        out_shape=(table(cells + STAT_ROWS),) * 2,
        compiler_params=params(),
    )(flat)
    edge_same, edge_following = pl.pallas_call(
        functools.partial(edges_kernel, edges=edges, cols=cols),
        out_shape=(table(edges + STAT_ROWS),) * 2,
        scratch_shapes=[pltpu.VMEM((cells, LANES), jnp.float32)],
        compiler_params=params(),
    )(flat, gn_gain.reshape(1, chans), gn_bias.reshape(1, chans))

    route_a, route_b, edge_a, edge_b = [], [], [], []
    for s in range(n_blocks):
        h = s // 2
        hops = [
            (route_a, edge_a, h, near_of(s), h),
            (route_a, edge_a, 1 - h, far_of(s), h),
            (route_b, edge_b, h, s, 1 - h),
            (route_b, edge_b, 1 - h, mid_of(s), 1 - h),
        ]
        for route, edge_route, core, there, core_there in hops:
            route.append((2 * s + core, 2 * there + core_there))
            for x in range(2):
                edge_route.append((4 * s + 2 * x + core, 4 * there + 2 * (1 - x) + core_there))
    swap = [(0, 1), (1, 0)]
    both = ("tm", "chan")
    got_b = lax.ppermute(same, both, route_b)
    got_a = lax.ppermute(following, both, route_a)
    got_edge_b = lax.ppermute(edge_same, ("tm", "tile", "chan"), edge_b)
    got_edge_a = lax.ppermute(edge_following, ("tm", "tile", "chan"), edge_a)

    received = (got_a, got_edge_a, got_b, got_edge_b)
    joined = pl.pallas_call(
        join_kernel,
        out_shape=table(sum(part.shape[0] for part in received)),
        compiler_params=params(),
    )(*received)
    swapped = lax.ppermute(joined, "chan", swap)

    def spread_out(n_frames, first, after=None):
        head = same if after is None else lax.optimization_barrier((same, after))[0]
        return pl.pallas_call(
            functools.partial(
                spread_kernel, frames=frames, rows=rows, cols=cols, entries=entries, first=first
            ),
            out_shape=jax.ShapeDtypeStruct((3, n_frames, rows + 2, cols, LANES), jnp.bfloat16),
            scratch_shapes=[pltpu.VMEM(same.shape, jnp.bfloat16)],
            compiler_params=params(),
        )(head, *received, swapped)

    narrow = spread_out(2 + frames, True)

    weight = conv_weight.reshape(27 * LANES, outs)
    bias = conv_bias.reshape(1, outs)

    def partial_sums(acts, jobs, spans, adds=(), with_bias=False, dtype=jnp.bfloat16, after=None, cost=1):
        source = acts if after is None else lax.optimization_barrier((acts, after))[0]
        return pl.pallas_call(
            functools.partial(
                partial_kernel,
                jobs=jobs,
                n_adds=len(adds),
                n_outs=len(spans),
                frames=frames,
                rows=rows,
                cols=cols,
                with_bias=with_bias,
            ),
            out_shape=[jax.ShapeDtypeStruct((n * rows * cols, outs), dtype) for n in spans],
            compiler_params=params(),
            cost_estimate=pl.CostEstimate(flops=cost, transcendentals=0, bytes_accessed=1),
        )(source, weight, *adds, *([bias] if with_bias else []))

    def mixed(core, ours, theirs):
        return lambda s: jnp.where(lax.axis_index("chan") == core, ours(s), theirs(s))

    def frame(block_of, f):
        return lambda s: block_of(s) * frames + f

    def route(core, goal):
        return [
            (2 * s + c, 2 * (goal(s) if c == core else near_of(s)) + c)
            for s in range(n_blocks)
            for c in range(2)
        ]

    lead = partial_sums(narrow, [(mixed(0, lambda s: 0, lambda s: 1), 0, 0, ())], [1], cost=1 << 32)
    spread = spread_out(2 + n_blocks * frames, False, lead[0])
    second = mixed(1, frame(far_of, 0), frame(mid_of, 1))
    second = partial_sums(spread, [(second, 0, 0, ())], [1], after=lead, cost=1 << 32)
    jobs = [(mixed(core, frame(mid_of, 0), frame(near_of, 0)), 1 - core, 0, ()) for core in range(2)]
    straight = partial_sums(spread, jobs, [1, 1], after=second, cost=1 << 32)
    got_1 = lax.ppermute(lead[0], both, route(0, far_of))
    got_2 = lax.ppermute(second[0], both, route(1, far_of))
    got_3 = lax.ppermute(straight[0], both, route(1, mid_of))
    got_4 = lax.ppermute(straight[1], both, route(0, mid_of))
    last = [
        partial_sums(
            spread, [(mixed(core, frame(far_of, 1), frame(near_of, 1)), 0, 0, ((0, core),))], [1], (got,), after=after
        )[0]
        for core, got, after in ((0, got_2, straight), (1, got_1, got_2))
    ]
    got_5, got_6 = [lax.ppermute(sent, both, route(core, far_of)) for core, sent in enumerate(last)]
    home = []
    for f, adds, added in (
        (0, (got_1, got_2, got_3, got_4), ((0, 0), (1, 1), (2, None), (3, None))),
        (1, (), ()),
    ):
        jobs = [(frame(lambda s: s, f), 0, 0, added)]
        after = home or None
        home += partial_sums(spread, jobs, [1], adds, True, jnp.float32, after=after, cost=1 << 35)
    span = rows * cols
    whole = pl.pallas_call(
        place_kernel,
        grid=(1,),
        in_specs=[pl.BlockSpec((span, outs), lambda i: (0, 0))],
        out_specs=pl.BlockSpec((span, outs), lambda i: (0, 0)),
        out_shape=jax.ShapeDtypeStruct((cells, outs), jnp.bfloat16),
        compiler_params=params(),
    )(home[0])
    result = pl.pallas_call(
        finish_kernel,
        grid=(1,),
        in_specs=[pl.BlockSpec(memory_space=pl.ANY)] + [pl.BlockSpec((span, outs), lambda i: (0, 0))] * 3,
        out_specs=pl.BlockSpec((span, outs), lambda i: (1, 0)),
        out_shape=jax.ShapeDtypeStruct((cells, outs), jnp.bfloat16),
        input_output_aliases={0: 0},
        compiler_params=params(),
    )(whole, home[1], got_5, got_6)
    return result.reshape(frames, rows, cols, outs)


def splits(mesh):
    size = mesh.shape
    return size["tm"] == 4 and size["tile"] == 2 and size["chan"] == 2 and CH == size["tm"] * LANES


def solution(mesh):
    in_specs = (
        P(("groups", "tm"), None, "tile", "chan"),
        P("chan"),
        P("chan"),
        P(None, "tm", "chan"),
        P("chan"),
    )
    out_specs = P(("groups", "tm"), None, "tile", "chan")
    chosen = split_body if splits(mesh) else body
    return jax.shard_map(chosen, mesh=mesh, in_specs=in_specs, out_specs=out_specs, check_vma=False)
```
